512 devices in a mesh: feat: 64 (over x, z), dom: 8 (over y, core).
Axes of the slice: x: 4, y: 4, z: 16, core: 2. Of those that a mesh axis runs over, the one named last changes fastest.
Arguments:
- features: bfloat16 [65536, 1024], P('dom', 'feat'), may hold values from -6 to 6
- self_weight: bfloat16 [1024, 512], P('feat'), may hold values from -0.1875 to 0.1875
- neighbour_weight: bfloat16 [1024, 512], P('feat'), may hold values from -1.5 to 1.5
- cotangent: bfloat16 [65536, 512], P(('dom', 'feat')), may hold values from -0.09375 to 0.09375
- send_rows: int32 [8, 8, 256], replicated, may hold values from 0 to 8191
- send_count: int32 [8, 8], replicated, may hold values from 32 to 256, as said below
- tile_source: int32 [8, 64, 8], P('dom'), may hold values from 0 to 79
- tile_kind: int32 [8, 64, 8], P('dom'), may hold values from 0 to 63
- tile_patterns: bfloat16 [64, 128, 128], replicated, may hold values from 0.0099487305 to 1
Outputs:
- hidden: bfloat16 [65536, 512], P(('dom', 'feat'))
- grad_self: float32 [1024, 512], P('feat')
- grad_neighbour: float32 [1024, 512], P('feat')
The draws below stay inside these ranges and needn't reach their ends.
Inputs may be any that keep to these rules, and one draw needn't show every extreme that they name: `send_count`: one destination has 256 live slots from every owner.
All inputs are finite; a program needn't handle non-finite values.
Results may differ from the reference program's by a relative error of at most 0.005.
Values may be sent and summed in bfloat16 or wider, within the bound.
A program may use at most 128 MiB of HBM per device.

```python
import math
import jax
import jax.numpy as jnp
from jax import lax

D_IN = 1024
HID = 512
TILE = 128
K = 8
NBANK = 64
CAP = 256
P_SIZE = 8192
NPART = 8
HALO = 2048
NODES = 65536


def draw_send_count(key, part):
    base = jax.random.randint(jax.random.fold_in(key, 11), (NPART, NPART), CAP // 8, CAP + 1)
    full_dest = jax.random.randint(jax.random.fold_in(key, 13), (), 0, NPART)
    dests = jnp.arange(NPART, dtype=jnp.int32)
    full = jnp.broadcast_to(dests[None, :] == full_dest, (NPART, NPART))
    return jnp.where(full, CAP, base).astype(jnp.int32)


def with_ends(array, own_key, least, top_value):
    shape = array.shape
    place = [jax.random.randint(jax.random.fold_in(own_key, axis), (), 0, shape[axis]) for axis in range(len(shape))]
    array = array.at[tuple(place)].set(least)
    longest = shape.index(max(shape))
    place[longest] = (place[longest] + 1) % shape[longest]
    return array.at[tuple(place)].set(top_value)


def steps_of(own_key, extent, cuts, smallest, top_value):
    def one(axis_at, parts):
        steps = jax.random.uniform(jax.random.fold_in(jax.random.fold_in(own_key, 6), axis_at), (parts,), jnp.float32, smallest / len(cuts), top_value / len(cuts))
        return jnp.repeat(jnp.exp(steps), extent[axis_at] // parts).reshape((-1,) + (1,) * (len(extent) - axis_at - 1))

    factor_of = one(*cuts[0])
    for cut in cuts[1:]:
        factor_of = factor_of * one(*cut)
    return factor_of


def bell_draw(rng, dims, scale, reach, cuts=(), kind=jnp.bfloat16):
    result = jax.random.normal(rng, dims, jnp.float32) * scale
    if len(cuts) > 0:
        result = steps_of(rng, dims, cuts, -0.22, 0.18) * result
    return jnp.clip(result, min=-reach, max=reach).astype(kind)


def setup_inputs(seed: int = 0) -> dict:
    streams_of = jax.random.split(jax.random.key(seed), 10)
    features = bell_draw(streams_of[0], (NODES, D_IN), 1.0, 6.0, ((0, 8), (1, 64)))
    self_weight = bell_draw(streams_of[1], (D_IN, HID), D_IN ** -0.5, 0.1875, ((0, 64),))
    neighbour_weight = bell_draw(streams_of[2], (D_IN, HID), 0.25, 1.5, ((0, 64),))
    cotangent = bell_draw(streams_of[3], (NODES, HID), (NODES // 16) ** -0.5, 0.09375, ((0, 512),))
    send_rows = with_ends(jax.random.randint(streams_of[4], (NPART, NPART, CAP), 0, P_SIZE), jax.random.fold_in(streams_of[4], 1), 0, P_SIZE - 1).astype(jnp.int32)
    send_count = draw_send_count(jax.random.fold_in(streams_of[9], 71), 0)
    tile_source = with_ends(jax.random.randint(streams_of[6], (NPART, P_SIZE // TILE, K), 0, (P_SIZE + HALO) // TILE), jax.random.fold_in(streams_of[6], 1), 0, ((P_SIZE + HALO) // TILE) - 1).astype(jnp.int32)
    tile_kind = with_ends(jax.random.randint(streams_of[7], (NPART, P_SIZE // TILE, K), 0, NBANK), jax.random.fold_in(streams_of[7], 1), 0, NBANK - 1).astype(jnp.int32)
    tile_patterns = jnp.clip(jnp.exp(jax.random.uniform(streams_of[8], (NBANK, TILE, TILE), jnp.float32, math.log(0.0099487305), math.log(1.0))), 0.0099487305, 1.0).astype(jnp.bfloat16)
    return dict(features=features, self_weight=self_weight, neighbour_weight=neighbour_weight, cotangent=cotangent, send_rows=send_rows, send_count=send_count, tile_source=tile_source, tile_kind=tile_kind, tile_patterns=tile_patterns)


inv_root_two = 0.7071067811865476
inv_root_two_pi = 0.3989422804014327


def gelu_pair(linear):
    normal_cdf = 0.5 * (1.0 + jax.scipy.special.erf(linear * inv_root_two))
    density = jnp.exp(-0.5 * linear * linear) * inv_root_two_pi
    return linear * normal_cdf, normal_cdf + linear * density


def partition_mean(features, send_rows, send_count, tile_source, tile_kind, tile_patterns, part_index):
    owners = jnp.arange(NPART, dtype=jnp.int32)
    wanted = send_rows[:, part_index, :]
    flat_ids = (owners[:, None] * P_SIZE + wanted).reshape(-1).astype(jnp.int32)
    live_mask = (jnp.arange(CAP, dtype=jnp.int32)[None, :] < send_count[:, part_index][:, None]).reshape(-1)
    halo = jnp.where(live_mask[:, None], features[flat_ids], jnp.zeros((), jnp.bfloat16))
    local_rows = lax.dynamic_slice_in_dim(features, part_index * P_SIZE, P_SIZE, 0)
    extended = jnp.concatenate([local_rows, halo], 0).reshape(-1, TILE, D_IN)
    tile_mats = tile_patterns[tile_kind[part_index]].astype(jnp.float32)
    sources = extended[tile_source[part_index]].astype(jnp.float32)
    summed = jnp.einsum("tkab,tkbf->taf", tile_mats, sources)
    degree = jnp.sum(tile_mats, axis=(1, 3))
    return (summed / degree[:, :, None]).reshape(P_SIZE, D_IN).astype(jnp.bfloat16)


def reference(features, self_weight, neighbour_weight, cotangent, send_rows, send_count, tile_source, tile_kind, tile_patterns):
    pieces = []
    for part_index in range(NPART):
        pieces.append(partition_mean(features, send_rows, send_count, tile_source, tile_kind, tile_patterns, part_index))
    neighbour_mean = jnp.concatenate(pieces, 0)
    linear = jnp.dot(features, self_weight, preferred_element_type=jnp.float32) + jnp.dot(neighbour_mean, neighbour_weight, preferred_element_type=jnp.float32)
    gelu_value, gelu_slope = gelu_pair(linear)
    hidden = gelu_value.astype(jnp.bfloat16)
    grad_linear = (cotangent.astype(jnp.float32) * gelu_slope).astype(jnp.bfloat16)
    grad_self = jnp.dot(features.T, grad_linear, preferred_element_type=jnp.float32)
    grad_neighbour = jnp.dot(neighbour_mean.T, grad_linear, preferred_element_type=jnp.float32)
    return hidden, grad_self, grad_neighbour
```

```python
import jax
import jax.numpy as jnp
from jax import lax
from jax.experimental import pallas as pl
from jax.experimental.pallas import tpu as pltpu
from jax.sharding import PartitionSpec as P

FEAT_GRID = (4, 16)
DOM_GRID = (4, 2)
inv_root_two = 0.7071067811865476
inv_root_two_pi = 0.3989422804014327
BF = jnp.bfloat16
F32 = jnp.float32
MESH = pl.DeviceIdType.MESH


def gelu_pair(linear):
    normal_cdf = 0.5 * (1.0 + lax.erf(linear * inv_root_two))
    density = jnp.exp(-0.5 * linear * linear) * inv_root_two_pi
    return linear * normal_cdf, normal_cdf + linear * density


def drain(ref, sem):
    pltpu.make_async_copy(ref, ref, sem).wait()


def layer(
    x_ref, w1_ref, w2_ref, cot_ref, rows_ref, pat_ref, count_ref, source_ref, kind_ref,
    hid_ref, gs_ref, gn_ref,
    ext, halo_out, mean, xm, weights, grad, other, other_in, part, part_in, kept,
    column, column_in, cell, cell_in, final,
    sem_out, sem_in, core_sem, y_sem,
):
    nx, nz = FEAT_GRID
    ny, nc = DOM_GRID
    nf, nd = nx * nz, ny * nc
    feat = lax.axis_index("feat")
    dom = lax.axis_index("dom")
    x, z = feat // nz, feat % nz
    y, core = dom // nc, dom % nc
    width = x_ref.shape[0]
    depth = nf * width
    band = nz * width
    tiles = nf
    slot_tiles = halo_out.shape[1]
    slots = rows_ref.shape[2]
    steps = source_ref.shape[0]

    def send(src, dst, phase, where, recv=None):
        pltpu.make_async_remote_copy(
            src_ref=src, dst_ref=dst, send_sem=sem_out.at[phase],
            recv_sem=sem_in.at[phase] if recv is None else recv,
            device_id=where, device_id_type=MESH,
        ).start()

    def feat_at(fx, fz):
        return {"feat": fx * nz + fz, "dom": dom}

    def dom_at(dy, dc):
        return {"feat": feat, "dom": dy * nc + dc}

    barrier = pltpu.get_barrier_semaphore()

    def greet_feat(i, _):
        pl.semaphore_signal(
            barrier, inc=1, device_id={"feat": (feat + i) % nf, "dom": dom}, device_id_type=MESH
        )
        return 0

    def greet_dom(i, _):
        pl.semaphore_signal(
            barrier, inc=1, device_id={"feat": feat, "dom": (dom + i) % nd}, device_id_type=MESH
        )
        return 0

    lax.fori_loop(1, nf, greet_feat, 0)
    lax.fori_loop(1, nd, greet_dom, 0)

    def take(t, _):
        ext[t] = x_ref[:, pl.ds(pl.multiple_of(t * 128, 128), 128)]
        return 0

    lax.fori_loop(0, tiles, take, 0)
    xm[0, feat] = ext[feat]
    block = pl.ds(pl.multiple_of(y * 128, 128), 128)
    weights[core, y, x, z] = jnp.where(core == 0, w1_ref[:, block], w2_ref[:, block])
    pl.semaphore_wait(barrier, nf - 1 + nd - 1)

    def weights_z(i, _):
        there = weights.at[core, y, x, z]
        send(there, there, 0, feat_at(x, (z + i) % nz))
        return 0

    lax.fori_loop(1, nz, weights_z, 0)

    def features_out(i, _):
        peer = (feat + i) % nf
        send(ext.at[peer], xm.at[0, feat], 1, {"feat": peer, "dom": dom})
        return 0

    lax.fori_loop(1, nf, features_out, 0)

    group = min(tiles, 16)
    lane_ids = lax.broadcasted_iota(jnp.int32, (128, slots), 0)
    slot_ids = lax.broadcasted_iota(jnp.int32, (1, slots), 1)

    def pick(dest):
        wanted = rows_ref[dom, pl.ds(dest, 1), :]
        low, high = wanted & 127, wanted >> 7
        choose = jnp.where(lane_ids == low, 1.0, 0.0).astype(BF)
        found = jnp.zeros((width, slots), F32)
        for g in range(0, tiles, group):
            rows = ext[g : g + group].reshape(group * width, 128)
            spread = jnp.dot(rows, choose, preferred_element_type=F32)
            for h in range(group):
                found = jnp.where(
                    high == g + h, spread[h * width : (h + 1) * width], found
                )
        live = slot_ids < count_ref[dom, dest]
        return jnp.where(live, found, 0.0).astype(BF)

    def halo_send(i, _):
        dest = (dom + i) % nd
        found = pick(dest)
        for j in range(slot_tiles):
            halo_out[dest, j] = found[:, j * 128 : (j + 1) * 128]
        send(
            halo_out.at[dest], ext.at[pl.ds(tiles + dom * slot_tiles, slot_tiles)], 2,
            {"feat": feat, "dom": dest},
        )
        return 0

    lax.fori_loop(1, nd, halo_send, 0)
    found = pick(dom)
    for j in range(slot_tiles):
        ext[tiles + dom * slot_tiles + j] = found[:, j * 128 : (j + 1) * 128]

    drain(weights.at[core, y, x, pl.ds(0, nz - 1)], sem_in.at[0])

    def weights_x(i, _):
        there = weights.at[core, y, x]
        send(there, there, 3, feat_at((x + i) % nx, z))
        return 0

    lax.fori_loop(1, nx, weights_x, 0)
    drain(ext.at[pl.ds(tiles, (nd - 1) * slot_tiles)], sem_in.at[2])
    drain(weights.at[core, y, pl.ds(0, nx - 1)], sem_in.at[3])

    def weights_y(i, _):
        there = weights.at[core, y]
        send(there, there, 4, dom_at((y + i) % ny, core))
        return 0

    lax.fori_loop(1, ny, weights_y, 0)

    ones = jnp.ones((width, 256), BF)

    def mean_of(t):
        total = jnp.zeros((2 * width, 128), F32)
        for k in range(0, steps, 2):
            left = jnp.concatenate([ext[source_ref[k, t]], ext[source_ref[k + 1, t]]], axis=1)
            right = jnp.concatenate([pat_ref[kind_ref[k, t]], pat_ref[kind_ref[k + 1, t]]], axis=1)
            total = total + lax.dot_general(
                jnp.concatenate([left, ones], axis=0), right, (((1,), (1,)), ((), ())),
                preferred_element_type=F32,
            )
        return (total[:width] / total[width : width + 1]).astype(BF)

    def mean_out(i, _):
        peer = (feat + i) % nf
        mean[peer] = mean_of(peer)
        send(mean.at[peer], xm.at[1, feat], 5, {"feat": peer, "dom": dom})
        return 0

    lax.fori_loop(1, nf, mean_out, 0)
    xm[1, feat] = mean_of(feat)

    drain(weights.at[core, pl.ds(0, ny - 1)], sem_in.at[4])
    send(weights.at[core], weights.at[core], 6, dom_at(y, 1 - core))
    drain(xm.at[0, pl.ds(0, nf - 1)], sem_in.at[1])
    drain(weights.at[core], sem_in.at[6])
    drain(xm.at[1, pl.ds(0, nf - 1)], sem_in.at[5])

    own = [xm[m].reshape(depth, 128) for m in range(2)]
    for b in range(ny):
        span = slice(b * 128, (b + 1) * 128)
        linear = jnp.zeros((128, 128), F32)
        for m in range(2):
            linear = linear + lax.dot_general(
                own[m], weights[m, b].reshape(depth, 128), (((0,), (0,)), ((), ())),
                preferred_element_type=F32,
            )
        value, slope = gelu_pair(linear)
        hid_ref[:, span] = value.astype(BF)
        grad[:, span] = (cot_ref[:, span].astype(F32) * slope).astype(BF)

    def product(m, b):
        return jnp.dot(
            xm[m, pl.ds(b * nz, nz)].reshape(band, 128), grad[...], preferred_element_type=F32
        )

    def core_out(i, _):
        b = (x + i) % nx
        result = product(1 - core, b).astype(BF)
        for c in range(ny):
            other[b, c] = result[:, c * 128 : (c + 1) * 128]
        send(other.at[b], other_in.at[b], 7, dom_at(y, 1 - core), core_sem.at[b])
        return 0

    lax.fori_loop(1, nx + 1, core_out, 0)

    def y_out(i, _):
        b = (x + i) % nx
        result = product(core, b)
        drain(other_in.at[b], core_sem.at[b])
        for c in range(ny):
            summed = result[:, c * 128 : (c + 1) * 128] + other_in[b, c].astype(F32)
            part[b, c] = summed.astype(BF)

            @pl.when(c == y)
            def _():
                kept[b] = summed

        def one(j, _):
            c = (y + j) % ny
            send(part.at[b, c], part_in.at[b, y], 8, dom_at(c, core), y_sem.at[b])
            return 0

        lax.fori_loop(1, ny, one, 0)
        return 0

    lax.fori_loop(1, nx + 1, y_out, 0)

    def y_sum(b):
        drain(part_in.at[b, pl.ds(0, ny - 1)], y_sem.at[b])
        total = kept[b]
        for j in range(1, ny):
            total = total + part_in[b, (y + j) % ny].astype(F32)
        return total

    def x_out(i, _):
        b = (x + i) % nx
        column[b] = y_sum(b).astype(BF)
        send(column.at[b], column_in.at[x], 9, feat_at(b, z))
        return 0

    lax.fori_loop(1, nx, x_out, 0)
    total = y_sum(x)
    drain(column_in.at[pl.ds(0, nx - 1)], sem_in.at[9])
    for j in range(1, nx):
        total = total + column_in[(x + j) % nx].astype(F32)

    kept[x] = total
    cell[...] = total.astype(BF).reshape(nz, width, 128)

    def z_out(i, _):
        peer = (z + i) % nz
        send(cell.at[peer], cell_in.at[z], 10, feat_at(x, peer))
        return 0

    lax.fori_loop(1, nz, z_out, 0)
    drain(cell_in.at[pl.ds(0, nz - 1)], sem_in.at[10])
    total = kept[x, pl.ds(pl.multiple_of(z * width, width), width)]
    for j in range(1, nz):
        total = total + cell_in[(z + j) % nz].astype(F32)

    final[dom] = total

    def dom_out(i, _):
        send(final.at[dom], final.at[dom], 11, {"feat": feat, "dom": (dom + i) % nd})
        return 0

    lax.fori_loop(1, nd, dom_out, 0)
    drain(final.at[pl.ds(0, nd - 1)], sem_in.at[11])
    for b in range(ny):
        span = slice(b * 128, (b + 1) * 128)
        gs_ref[:, span] = final[b * nc]
        gn_ref[:, span] = final[b * nc + 1]

    drain(weights.at[core, y, x, pl.ds(0, nz - 1)], sem_out.at[0])
    drain(ext.at[pl.ds(0, nf - 1)], sem_out.at[1])
    drain(halo_out.at[pl.ds(0, nd - 1)], sem_out.at[2])
    drain(weights.at[core, y, pl.ds(0, nx - 1)], sem_out.at[3])
    drain(weights.at[core, pl.ds(0, ny - 1)], sem_out.at[4])
    drain(mean.at[pl.ds(0, nf - 1)], sem_out.at[5])
    drain(weights.at[core], sem_out.at[6])
    drain(other, sem_out.at[7])
    drain(part.at[:, pl.ds(0, ny - 1)], sem_out.at[8])
    drain(column.at[pl.ds(0, nx - 1)], sem_out.at[9])
    drain(cell.at[pl.ds(0, nz - 1)], sem_out.at[10])
    drain(final.at[pl.ds(0, nd - 1)], sem_out.at[11])


def on_device(features, w1, w2, cotangent, send_rows, send_count, tile_source, tile_kind, patterns):
    nx, nz = FEAT_GRID
    ny, nc = DOM_GRID
    nf, nd = nx * nz, ny * nc
    width = features.shape[1]
    hidden = w1.shape[1]
    slot_tiles = send_rows.shape[2] // 128
    assert features.shape[0] == nf * 128 and hidden == ny * 128 and nc == 2
    band = nz * width
    vmem = pl.BlockSpec(memory_space=pltpu.VMEM)
    smem = pl.BlockSpec(memory_space=pltpu.SMEM)
    return pl.pallas_call(
        layer,
        out_shape=(
            jax.ShapeDtypeStruct((128, hidden), BF),
            jax.ShapeDtypeStruct((width, hidden), F32),
            jax.ShapeDtypeStruct((width, hidden), F32),
        ),
        in_specs=[vmem] * 6 + [smem] * 3,
        out_specs=(vmem,) * 3,
        scratch_shapes=[
            pltpu.VMEM((nf + nd * slot_tiles, width, 128), BF),
            pltpu.VMEM((nd, slot_tiles, width, 128), BF),
            pltpu.VMEM((nf, width, 128), BF),
            pltpu.VMEM((2, nf, width, 128), BF),
            pltpu.VMEM((nc, ny, nx, nz, width, 128), BF),
            pltpu.VMEM((128, hidden), BF),
            pltpu.VMEM((nx, ny, band, 128), BF),
            pltpu.VMEM((nx, ny, band, 128), BF),
            pltpu.VMEM((nx, ny, band, 128), BF),
            pltpu.VMEM((nx, ny, band, 128), BF),
            pltpu.VMEM((nx, band, 128), F32),
            pltpu.VMEM((nx, band, 128), BF),
            pltpu.VMEM((nx, band, 128), BF),
            pltpu.VMEM((nz, width, 128), BF),
            pltpu.VMEM((nz, width, 128), BF),
            pltpu.VMEM((nd, width, 128), F32),
            pltpu.SemaphoreType.DMA((12,)),
            pltpu.SemaphoreType.DMA((12,)),
            pltpu.SemaphoreType.DMA((nx,)),
            pltpu.SemaphoreType.DMA((nx,)),
        ],
        compiler_params=pltpu.CompilerParams(
            collective_id=0, has_side_effects=True, vmem_limit_bytes=48 << 20
        ),
    )(
        features.T, w1, w2, cotangent, send_rows, patterns, send_count,
        tile_source[0].T, tile_kind[0].T,
    )


def solution(mesh):
    placed = (
        P("dom", "feat"),
        P("feat", None),
        P("feat", None),
        P(("dom", "feat"), None),
        P(),
        P(),
        P("dom", None, None),
        P("dom", None, None),
        P(),
    )
    return jax.shard_map(
        on_device,
        mesh=mesh,
        in_specs=placed,
        out_specs=(P(("dom", "feat"), None), P("feat", None), P("feat", None)),
        check_vma=False,
    )
```

```python
import jax
import jax.numpy as jnp
from jax import lax
from jax.experimental import pallas as pl
from jax.experimental.pallas import tpu as pltpu
from jax.sharding import PartitionSpec as P

FEAT_GRID = (4, 16)
DOM_GRID = (4, 2)
inv_root_two = 0.7071067811865476
inv_root_two_pi = 0.3989422804014327
BF = jnp.bfloat16
F32 = jnp.float32
MESH = pl.DeviceIdType.MESH


def gelu_pair(linear):
    normal_cdf = 0.5 * (1.0 + lax.erf(linear * inv_root_two))
    density = jnp.exp(-0.5 * linear * linear) * inv_root_two_pi
    return linear * normal_cdf, normal_cdf + linear * density


def drain(ref, sem):
    pltpu.make_async_copy(ref, ref, sem).wait()


def layer(
    x_hbm, w1_hbm, w2_hbm, cot_hbm, rows_hbm, pat_hbm, count_hbm, source_hbm, kind_hbm,
    hid_ref, gs_ref, gn_ref,
    x_own, wanted_ref, pats, cot, count_ref, source_ref, kind_ref,
    ext, halo_out, mean, xm, weights, partial, grad, other, other_in,
    part_a, part_a_in, part_b, part_b_in, kept_a, kept_b,
    col_a, col_a_in, col_b, col_b_in, fin, cell, cell_in, final,
    sem_out, sem_in, load_sem,
):
    nx, nz = FEAT_GRID
    ny, nc = DOM_GRID
    nf, nd, hz = nx * nz, ny * nc, nz // 2
    feat = lax.axis_index("feat")
    dom = lax.axis_index("dom")
    x, z = feat // nz, feat % nz
    y, core = dom // nc, dom % nc
    half, zz = z // hz, z % hz
    slot = half * (nx * hz) + x * hz + zz
    width = x_own.shape[0]
    depth = nx * hz * width
    band = hz * width
    tiles = nf
    slot_tiles = halo_out.shape[1]
    slots = wanted_ref.shape[1]
    steps = source_ref.shape[0]

    def send(src, dst, phase, where):
        pltpu.make_async_remote_copy(
            src_ref=src, dst_ref=dst, send_sem=sem_out.at[phase], recv_sem=sem_in.at[phase],
            device_id=where, device_id_type=MESH,
        ).start()

    def feat_at(fx, fz):
        return {"feat": fx * nz + fz, "dom": dom}

    def dom_at(dy, dc):
        return {"feat": feat, "dom": dy * nc + dc}

    block = pl.ds(pl.multiple_of(y * 128, 128), 128)
    my_unit = weights.at[half, core, y, x, zz]
    loads = [
        pltpu.make_async_copy(src, dst, load_sem.at[i])
        for i, (src, dst) in enumerate((
            (x_hbm, x_own), (rows_hbm.at[dom], wanted_ref), (count_hbm, count_ref),
            (pat_hbm, pats), (source_hbm, source_ref), (kind_hbm, kind_ref), (cot_hbm, cot),
        ))
    ]
    for load in loads:
        load.start()

    @pl.when(core == 0)
    def _():
        pltpu.make_async_copy(w1_hbm.at[:, block], my_unit, load_sem.at[7]).start()

    @pl.when(core == 1)
    def _():
        pltpu.make_async_copy(w2_hbm.at[:, block], my_unit, load_sem.at[7]).start()

    barrier = pltpu.get_barrier_semaphore()

    def greet_feat(i, _):
        pl.semaphore_signal(
            barrier, inc=1, device_id={"feat": (feat + i) % nf, "dom": dom}, device_id_type=MESH
        )
        return 0

    def greet_dom(i, _):
        pl.semaphore_signal(
            barrier, inc=1, device_id={"feat": feat, "dom": (dom + i) % nd}, device_id_type=MESH
        )
        return 0

    lax.fori_loop(1, nf, greet_feat, 0)
    lax.fori_loop(1, nd, greet_dom, 0)
    for load in loads[:3]:
        load.wait()

    def take(t, _):
        ext[t] = x_own[:, pl.ds(pl.multiple_of(t * 128, 128), 128)]
        return 0

    lax.fori_loop(0, tiles, take, 0)
    xm[0, slot] = ext[feat]

    group = min(tiles, 16)
    lane_ids = lax.broadcasted_iota(jnp.int32, (128, slots), 0)
    slot_ids = lax.broadcasted_iota(jnp.int32, (1, slots), 1)

    def pick(dest, _):
        wanted = wanted_ref[pl.ds(dest, 1), :]
        low, high = wanted & 127, wanted >> 7
        choose = jnp.where(lane_ids == low, 1.0, 0.0).astype(BF)
        found = jnp.zeros((width, slots), F32)
        for g in range(0, tiles, group):
            rows = ext[g : g + group].reshape(group * width, 128)
            spread = jnp.dot(rows, choose, preferred_element_type=F32)
            for h in range(group):
                found = jnp.where(
                    high == g + h, spread[h * width : (h + 1) * width], found
                )
        live = slot_ids < count_ref[dom, dest]
        found = jnp.where(live, found, 0.0).astype(BF)
        for j in range(slot_tiles):
            halo_out[dest, j] = found[:, j * 128 : (j + 1) * 128]
        return 0

    lax.fori_loop(0, nd, pick, 0)
    halo_at = tiles + dom * slot_tiles
    for j in range(slot_tiles):
        ext[halo_at + j] = halo_out[dom, j]
    pltpu.make_async_copy(my_unit, my_unit, load_sem.at[7]).wait()
    for load in loads[3:]:
        load.wait()
    pl.semaphore_wait(barrier, nf - 1 + nd - 1)

    def halo_send(i, _):
        dest = (dom + i) % nd
        send(
            halo_out.at[dest], ext.at[pl.ds(halo_at, slot_tiles)], 0,
            {"feat": feat, "dom": dest},
        )
        return 0

    lax.fori_loop(1, nd, halo_send, 0)

    def weights_z(i, _):
        send(my_unit, my_unit, 1, feat_at(x, (z + i) % nz))
        return 0

    lax.fori_loop(1, nz, weights_z, 0)

    def features_out(i, _):
        peer = (feat + i) % nf
        send(ext.at[peer], xm.at[0, slot], 2, {"feat": peer, "dom": dom})
        return 0

    lax.fori_loop(1, nf, features_out, 0)

    ones = jnp.ones((width, 256), BF)

    def mean_of(t):
        total = jnp.zeros((2 * width, 128), F32)
        for k in range(0, steps, 2):
            left = jnp.concatenate([ext[source_ref[k, t]], ext[source_ref[k + 1, t]]], axis=1)
            right = jnp.concatenate([pats[kind_ref[k, t]], pats[kind_ref[k + 1, t]]], axis=1)
            total = total + lax.dot_general(
                jnp.concatenate([left, ones], axis=0), right, (((1,), (1,)), ((), ())),
                preferred_element_type=F32,
            )
        return (total[:width] / total[width : width + 1]).astype(BF)

    def mean_out(i, _):
        peers = [(feat + 1 + 2 * i + j) % nf for j in range(2)]
        found = [mean_of(peer) for peer in peers]
        for peer, value in zip(peers, found):
            mean[peer] = value
        for peer in peers:

            @pl.when(peer != feat)
            def _():
                send(mean.at[peer], xm.at[1, slot], 3, {"feat": peer, "dom": dom})

        return 0

    drain(ext.at[pl.ds(tiles, (nd - 1) * slot_tiles)], sem_in.at[0])
    lax.fori_loop(0, nf // 2, mean_out, 0)
    xm[1, slot] = mean[feat]

    drain(ext.at[pl.ds(0, nz - 1)], sem_in.at[1])
    first_a, first_b = weights.at[0, core, y, x], weights.at[1, core, y, x]
    for i in range(1, nx):
        send(first_a, first_a, 4, feat_at((x + i) % nx, z))
    for i in range(1, ny):
        send(first_b, first_b, 5, dom_at((y + i) % ny, core))
    drain(weights.at[0, core, y, pl.ds(0, nx - 1)], sem_in.at[4])
    then_a = weights.at[0, core, y]
    for i in range(1, ny):
        send(then_a, then_a, 6, dom_at((y + i) % ny, core))
    drain(weights.at[1, core, pl.ds(0, ny - 1), x], sem_in.at[5])
    then_b = weights.at[1, core, :, x]
    for i in range(1, nx):
        send(then_b, then_b, 7, feat_at((x + i) % nx, z))
    drain(weights.at[0, core, pl.ds(0, ny - 1)], sem_in.at[6])
    drain(weights.at[1, core, :, pl.ds(0, nx - 1)], sem_in.at[7])
    for h in range(2):
        send(weights.at[h, core], weights.at[h, core], 8, dom_at(y, 1 - core))
    drain(xm.at[0, pl.ds(0, nf - 1)], sem_in.at[2])

    def times_weights(m, own, b):
        total = jnp.zeros((128, 128), F32)
        for h in range(2):
            total = total + lax.dot_general(
                own[h], weights[h, m, b].reshape(depth, 128), (((0,), (0,)), ((), ())),
                preferred_element_type=F32,
            )
        return total

    def halves(m):
        return [xm[m, h * nx * hz : (h + 1) * nx * hz].reshape(depth, 128) for h in range(2)]

    drain(weights.at[0], sem_in.at[8])
    own = halves(0)
    for b in range(ny):
        partial[:, b * 128 : (b + 1) * 128] = times_weights(0, own, b)
    drain(xm.at[1, pl.ds(0, nf - 1)], sem_in.at[3])
    own = halves(1)
    for b in range(ny):
        span = slice(b * 128, (b + 1) * 128)
        value, slope = gelu_pair(partial[:, span] + times_weights(1, own, b))
        hid_ref[:, span] = value.astype(BF)
        grad[:, span] = (cot[:, span].astype(F32) * slope).astype(BF)

    def product(m, h, b):
        rows = xm[m, pl.ds(h * nx * hz + b * hz, hz)].reshape(band, 128)
        return jnp.dot(rows, grad[...], preferred_element_type=F32)

    for h in range(2):

        def core_out(b, _, h=h):
            result = product(1 - core, h, b).astype(BF)
            for c in range(ny):
                other[h, b, c] = result[:, c * 128 : (c + 1) * 128]
            return 0

        lax.fori_loop(0, nx, core_out, 0)
        send(other.at[h], other_in.at[h], 9 + h, dom_at(y, 1 - core))

    drain(other_in.at[0], sem_in.at[9])

    def y_first(b, _):
        result = product(core, 0, b)
        for c in range(ny):
            summed = result[:, c * 128 : (c + 1) * 128] + other_in[0, b, c].astype(F32)
            part_a[c, b] = summed.astype(BF)

            @pl.when(c == y)
            def _():
                kept_a[b] = summed

        return 0

    lax.fori_loop(0, nx, y_first, 0)
    for i in range(1, ny):
        c = (y + i) % ny
        send(part_a.at[c], part_a_in.at[y], 11, dom_at(c, core))

    drain(other_in.at[1], sem_in.at[10])

    def x_first(b, _):
        result = product(core, 1, b)
        for c in range(ny):
            summed = result[:, c * 128 : (c + 1) * 128] + other_in[1, b, c].astype(F32)
            part_b[b, c] = summed.astype(BF)

            @pl.when(b == x)
            def _():
                kept_b[c] = summed

        return 0

    lax.fori_loop(0, nx, x_first, 0)
    for i in range(1, nx):
        b = (x + i) % nx
        send(part_b.at[b], part_b_in.at[x], 12, feat_at(b, z))

    def y_sum(b):
        total = kept_a[b]
        for j in range(1, ny):
            total = total + part_a_in[(y + j) % ny, b].astype(F32)
        return total

    def x_sum(c):
        total = kept_b[c]
        for j in range(1, nx):
            total = total + part_b_in[(x + j) % nx, c].astype(F32)
        return total

    drain(part_a_in.at[pl.ds(0, ny - 1)], sem_in.at[11])

    def x_then(i, _):
        b = (x + i) % nx
        col_a[b] = y_sum(b).astype(BF)
        send(col_a.at[b], col_a_in.at[x], 13, feat_at(b, z))
        return 0

    lax.fori_loop(1, nx, x_then, 0)
    fin[0] = y_sum(x)

    drain(part_b_in.at[pl.ds(0, nx - 1)], sem_in.at[12])

    def y_then(i, _):
        c = (y + i) % ny
        col_b[c] = x_sum(c).astype(BF)
        send(col_b.at[c], col_b_in.at[y], 14, dom_at(c, core))
        return 0

    lax.fori_loop(1, ny, y_then, 0)
    fin[1] = x_sum(y)

    def z_out(i, _):
        peer = i

        @pl.when(peer != z)
        def _():
            send(cell.at[peer], cell_in.at[z], 15, feat_at(x, peer))

        return 0

    drain(col_a_in.at[pl.ds(0, nx - 1)], sem_in.at[13])
    total = fin[0]
    for j in range(1, nx):
        total = total + col_a_in[(x + j) % nx].astype(F32)
    fin[0] = total
    cell[0:hz] = total.astype(BF).reshape(hz, width, 128)
    lax.fori_loop(0, hz, z_out, 0)
    drain(col_b_in.at[pl.ds(0, ny - 1)], sem_in.at[14])
    total = fin[1]
    for j in range(1, ny):
        total = total + col_b_in[(y + j) % ny].astype(F32)
    fin[1] = total
    cell[hz:nz] = total.astype(BF).reshape(hz, width, 128)
    lax.fori_loop(hz, nz, z_out, 0)
    drain(cell_in.at[pl.ds(0, nz - 1)], sem_in.at[15])
    total = fin[half, pl.ds(pl.multiple_of(zz * width, width), width)]
    for j in range(1, nz):
        total = total + cell_in[(z + j) % nz].astype(F32)

    final[dom] = total

    def dom_out(i, _):
        send(final.at[dom], final.at[dom], 16, {"feat": feat, "dom": (dom + i) % nd})
        return 0

    lax.fori_loop(1, nd, dom_out, 0)
    drain(final.at[pl.ds(0, nd - 1)], sem_in.at[16])
    for b in range(ny):
        span = slice(b * 128, (b + 1) * 128)
        gs_ref[:, span] = final[b * nc]
        gn_ref[:, span] = final[b * nc + 1]

    sent = (
        halo_out.at[pl.ds(0, nd - 1)], ext.at[pl.ds(0, nz - 1)], ext.at[pl.ds(0, nf - 1)],
        mean.at[pl.ds(0, nf - 1)], weights.at[0, core, y, pl.ds(0, nx - 1)],
        weights.at[1, core, pl.ds(0, ny - 1), x], weights.at[0, core, pl.ds(0, ny - 1)],
        weights.at[1, core, :, pl.ds(0, nx - 1)], weights.at[0], other.at[0], other.at[1],
        part_a.at[pl.ds(0, ny - 1)], part_b.at[pl.ds(0, nx - 1)],
        col_a.at[pl.ds(0, nx - 1)], col_b.at[pl.ds(0, ny - 1)], cell.at[pl.ds(0, nz - 1)],
        final.at[pl.ds(0, nd - 1)],
    )
    for phase, ref in enumerate(sent):
        drain(ref, sem_out.at[phase])


def store_out(hid_in, gs_in, gn_in, hid_ref, gs_ref, gn_ref, sems):
    pairs = ((hid_in, hid_ref), (gs_in, gs_ref), (gn_in, gn_ref))
    copies = [pltpu.make_async_copy(a, b, sems.at[i]) for i, (a, b) in enumerate(pairs)]
    for copy in copies:
        copy.start()
    for copy in copies:
        copy.wait()


def on_device(features, w1, w2, cotangent, send_rows, send_count, tile_source, tile_kind, patterns):
    nx, nz = FEAT_GRID
    ny, nc = DOM_GRID
    nf, nd, hz = nx * nz, ny * nc, nz // 2
    width = features.shape[1]
    hidden = w1.shape[1]
    slot_tiles = send_rows.shape[2] // 128
    assert features.shape[0] == nf * 128 and hidden == ny * 128 and nc == 2
    band = hz * width
    vmem = pl.BlockSpec(memory_space=pltpu.VMEM)
    hbm = pl.BlockSpec(memory_space=pltpu.HBM)
    source, kind = tile_source[0].T, tile_kind[0].T
    shapes = (
        jax.ShapeDtypeStruct((128, hidden), BF),
        jax.ShapeDtypeStruct((width, hidden), F32),
        jax.ShapeDtypeStruct((width, hidden), F32),
    )
    results = pl.pallas_call(
        layer,
        out_shape=shapes,
        in_specs=[hbm] * 9,
        out_specs=(vmem,) * 3,
        scratch_shapes=[
            pltpu.VMEM((width, nf * 128), BF),
            pltpu.VMEM(send_rows.shape[1:], jnp.int32),
            pltpu.VMEM(patterns.shape, BF),
            pltpu.VMEM((128, hidden), BF),
            pltpu.SMEM(send_count.shape, jnp.int32),
            pltpu.SMEM(source.shape, jnp.int32),
            pltpu.SMEM(kind.shape, jnp.int32),
            pltpu.VMEM((nf + nd * slot_tiles, width, 128), BF),
            pltpu.VMEM((nd, slot_tiles, width, 128), BF),
            pltpu.VMEM((nf, width, 128), BF),
            pltpu.VMEM((2, nf, width, 128), BF),
            pltpu.VMEM((2, nc, ny, nx, hz, width, 128), BF),
            pltpu.VMEM((128, hidden), F32),
            pltpu.VMEM((128, hidden), BF),
            pltpu.VMEM((2, nx, ny, band, 128), BF),
            pltpu.VMEM((2, nx, ny, band, 128), BF),
            pltpu.VMEM((ny, nx, band, 128), BF),
            pltpu.VMEM((ny, nx, band, 128), BF),
            pltpu.VMEM((nx, ny, band, 128), BF),
            pltpu.VMEM((nx, ny, band, 128), BF),
            pltpu.VMEM((nx, band, 128), F32),
            pltpu.VMEM((ny, band, 128), F32),
            pltpu.VMEM((nx, band, 128), BF),
            pltpu.VMEM((nx, band, 128), BF),
            pltpu.VMEM((ny, band, 128), BF),
            pltpu.VMEM((ny, band, 128), BF),
            pltpu.VMEM((2, band, 128), F32),
            pltpu.VMEM((nz, width, 128), BF),
            pltpu.VMEM((nz, width, 128), BF),
            pltpu.VMEM((nd, width, 128), F32),
            pltpu.SemaphoreType.DMA((17,)),
            pltpu.SemaphoreType.DMA((17,)),
            pltpu.SemaphoreType.DMA((8,)),
        ],
        compiler_params=pltpu.CompilerParams(
            collective_id=0, has_side_effects=True, vmem_limit_bytes=48 << 20
        ),
    )(
        features.T, w1, w2, cotangent, send_rows, patterns, send_count, source, kind,
    )
    anywhere = pl.BlockSpec(memory_space=pl.ANY)
    return pl.pallas_call(
        store_out,
        out_shape=shapes,
        in_specs=[anywhere] * 3,
        out_specs=(hbm,) * 3,
        scratch_shapes=[pltpu.SemaphoreType.DMA((3,))],
    )(*results)


def solution(mesh):
    placed = (
        P("dom", "feat"),
        P("feat", None),
        P("feat", None),
        P(("dom", "feat"), None),
        P(),
        P(),
        P("dom", None, None),
        P("dom", None, None),
        P(),
    )
    return jax.shard_map(
        on_device,
        mesh=mesh,
        in_specs=placed,
        out_specs=(P(("dom", "feat"), None), P("feat", None), P("feat", None)),
        check_vma=False,
    )
```

```python
import jax
import jax.numpy as jnp
from jax import lax
from jax.experimental import pallas as pl
from jax.experimental.pallas import tpu as pltpu
from jax.sharding import PartitionSpec as P

FEAT_GRID = (4, 16)
DOM_GRID = (4, 2)
inv_root_two = 0.7071067811865476
inv_root_two_pi = 0.3989422804014327
BF = jnp.bfloat16
F32 = jnp.float32
MESH = pl.DeviceIdType.MESH


def gelu_pair(linear):
    normal_cdf = 0.5 * (1.0 + lax.erf(linear * inv_root_two))
    density = jnp.exp(-0.5 * linear * linear) * inv_root_two_pi
    return linear * normal_cdf, normal_cdf + linear * density


def drain(ref, sem):
    pltpu.make_async_copy(ref, ref, sem).wait()


def layer(
    x_hbm, w1_hbm, w2_hbm, cot_hbm, rows_hbm, pat_hbm, count_hbm, source_hbm, kind_hbm,
    hid_ref, gs_ref, gn_ref,
    x_own, wanted_ref, pats, cot, count_ref, source_ref, kind_ref,
    ext, halo_out, mean, xm, weights, partial, grad, other, other_in,
    part_a, part_a_in, part_b, part_b_in, kept_a, kept_b,
    col_a, col_a_in, col_b, col_b_in, fin, cell, cell_in, final,
    sem_out, sem_in, load_sem,
):
    nx, nz = FEAT_GRID
    ny, nc = DOM_GRID
    nf, nd, hz = nx * nz, ny * nc, nz // 2
    feat = lax.axis_index("feat")
    dom = lax.axis_index("dom")
    x, z = feat // nz, feat % nz
    y, core = dom // nc, dom % nc
    half, zz = z // hz, z % hz
    slot = half * (nx * hz) + x * hz + zz
    width = x_own.shape[0]
    depth = nx * hz * width
    band = hz * width
    tiles = nf
    slot_tiles = halo_out.shape[1]
    slots = wanted_ref.shape[1]
    steps = source_ref.shape[0]

    def send(src, dst, phase, where):
        pltpu.make_async_remote_copy(
            src_ref=src, dst_ref=dst, send_sem=sem_out.at[phase], recv_sem=sem_in.at[phase],
            device_id=where, device_id_type=MESH,
        ).start()

    def feat_at(fx, fz):
        return {"feat": fx * nz + fz, "dom": dom}

    def dom_at(dy, dc):
        return {"feat": feat, "dom": dy * nc + dc}

    block = pl.ds(pl.multiple_of(y * 128, 128), 128)
    my_unit = weights.at[half, core, y, x, zz]
    loads = [
        pltpu.make_async_copy(src, dst, load_sem.at[i])
        for i, (src, dst) in enumerate((
            (x_hbm, x_own), (rows_hbm.at[dom], wanted_ref), (count_hbm, count_ref),
            (pat_hbm, pats), (source_hbm, source_ref), (kind_hbm, kind_ref), (cot_hbm, cot),
        ))
    ]
    for load in loads:
        load.start()

    @pl.when(core == 0)
    def _():
        pltpu.make_async_copy(w1_hbm.at[:, block], my_unit, load_sem.at[7]).start()

    @pl.when(core == 1)
    def _():
        pltpu.make_async_copy(w2_hbm.at[:, block], my_unit, load_sem.at[7]).start()

    barrier = pltpu.get_barrier_semaphore()

    def greet_feat(i, _):
        pl.semaphore_signal(
            barrier, inc=1, device_id={"feat": (feat + i) % nf, "dom": dom}, device_id_type=MESH
        )
        return 0

    def greet_dom(i, _):
        pl.semaphore_signal(
            barrier, inc=1, device_id={"feat": feat, "dom": (dom + i) % nd}, device_id_type=MESH
        )
        return 0

    lax.fori_loop(1, nf, greet_feat, 0)
    lax.fori_loop(1, nd, greet_dom, 0)
    for load in loads[:3]:
        load.wait()

    def take(t, _):
        ext[t] = x_own[:, pl.ds(pl.multiple_of(t * 128, 128), 128)]
        return 0

    lax.fori_loop(0, tiles, take, 0)
    xm[0, slot] = ext[feat]

    group = min(tiles, 16)
    lane_ids = lax.broadcasted_iota(jnp.int32, (128, slots), 0)
    slot_ids = lax.broadcasted_iota(jnp.int32, (1, slots), 1)

    def pick(dest, _):
        wanted = wanted_ref[pl.ds(dest, 1), :]
        low, high = wanted & 127, wanted >> 7
        choose = jnp.where(lane_ids == low, 1.0, 0.0).astype(BF)
        found = jnp.zeros((width, slots), F32)
        for g in range(0, tiles, group):
            rows = ext[g : g + group].reshape(group * width, 128)
            spread = jnp.dot(rows, choose, preferred_element_type=F32)
            for h in range(group):
                found = jnp.where(
                    high == g + h, spread[h * width : (h + 1) * width], found
                )
        live = slot_ids < count_ref[dom, dest]
        found = jnp.where(live, found, 0.0).astype(BF)
        for j in range(slot_tiles):
            halo_out[dest, j] = found[:, j * 128 : (j + 1) * 128]
        return 0

    lax.fori_loop(0, nd, pick, 0)
    halo_at = tiles + dom * slot_tiles
    for j in range(slot_tiles):
        ext[halo_at + j] = halo_out[dom, j]
    pltpu.make_async_copy(my_unit, my_unit, load_sem.at[7]).wait()
    for load in loads[3:]:
        load.wait()
    pl.semaphore_wait(barrier, nf - 1 + nd - 1)

    def halo_send(i, _):
        dest = (dom + i) % nd
        send(
            halo_out.at[dest], ext.at[pl.ds(halo_at, slot_tiles)], 0,
            {"feat": feat, "dom": dest},
        )
        return 0

    lax.fori_loop(1, nd, halo_send, 0)

    def weights_z(i, _):
        send(my_unit, my_unit, 1, feat_at(x, (z + i) % nz))
        return 0

    lax.fori_loop(1, nz, weights_z, 0)

    def features_out(i, _):
        peer = (feat + i) % nf
        send(ext.at[peer], xm.at[0, slot], 2, {"feat": peer, "dom": dom})
        return 0

    lax.fori_loop(1, nf, features_out, 0)

    ones = jnp.ones((width, 256), BF)

    def mean_of(t):
        total = jnp.zeros((2 * width, 128), F32)
        for k in range(0, steps, 2):
            left = jnp.concatenate([ext[source_ref[k, t]], ext[source_ref[k + 1, t]]], axis=1)
            right = jnp.concatenate([pats[kind_ref[k, t]], pats[kind_ref[k + 1, t]]], axis=1)
            total = total + lax.dot_general(
                jnp.concatenate([left, ones], axis=0), right, (((1,), (1,)), ((), ())),
                preferred_element_type=F32,
            )
        return (total[:width] / total[width : width + 1]).astype(BF)

    def mean_out(i, _):
        peers = [(feat + 1 + 2 * i + j) % nf for j in range(2)]
        found = [mean_of(peer) for peer in peers]
        for peer, value in zip(peers, found):
            mean[peer] = value
        for peer in peers:

            @pl.when(peer != feat)
            def _():
                send(mean.at[peer], xm.at[1, slot], 3, {"feat": peer, "dom": dom})

        return 0

    drain(ext.at[pl.ds(tiles, (nd - 1) * slot_tiles)], sem_in.at[0])
    lax.fori_loop(0, nf // 2, mean_out, 0)
    xm[1, slot] = mean[feat]

    drain(ext.at[pl.ds(0, nz - 1)], sem_in.at[1])
    first_a, first_b = weights.at[0, core, y, x], weights.at[1, core, y, x]
    for i in range(1, nx):
        send(first_a, first_a, 4, feat_at((x + i) % nx, z))
    for i in range(1, ny):
        send(first_b, first_b, 5, dom_at((y + i) % ny, core))
    drain(weights.at[0, core, y, pl.ds(0, nx - 1)], sem_in.at[4])
    then_a = weights.at[0, core, y]
    for i in range(1, ny):
        send(then_a, then_a, 6, dom_at((y + i) % ny, core))
    drain(weights.at[1, core, pl.ds(0, ny - 1), x], sem_in.at[5])
    then_b = weights.at[1, core, :, x]
    for i in range(1, nx):
        send(then_b, then_b, 7, feat_at((x + i) % nx, z))
    drain(weights.at[0, core, pl.ds(0, ny - 1)], sem_in.at[6])
    drain(weights.at[1, core, :, pl.ds(0, nx - 1)], sem_in.at[7])
    for h in range(2):
        send(weights.at[h, core], weights.at[h, core], 8, dom_at(y, 1 - core))
    drain(xm.at[0, pl.ds(0, nf - 1)], sem_in.at[2])

    def times_weights(m, own, b):
        total = jnp.zeros((128, 128), F32)
        for h in range(2):
            total = total + lax.dot_general(
                own[h], weights[h, m, b].reshape(depth, 128), (((0,), (0,)), ((), ())),
                preferred_element_type=F32,
            )
        return total

    def halves(m):
        return [xm[m, h * nx * hz : (h + 1) * nx * hz].reshape(depth, 128) for h in range(2)]

    drain(weights.at[0], sem_in.at[8])
    own = halves(0)
    for b in range(ny):
        partial[:, b * 128 : (b + 1) * 128] = times_weights(0, own, b)
    drain(xm.at[1, pl.ds(0, nf - 1)], sem_in.at[3])
    own = halves(1)
    for b in range(ny):
        span = slice(b * 128, (b + 1) * 128)
        value, slope = gelu_pair(partial[:, span] + times_weights(1, own, b))
        hid_ref[:, span] = value.astype(BF)
        grad[:, span] = (cot[:, span].astype(F32) * slope).astype(BF)

    def product(m, h, b):
        rows = xm[m, pl.ds(h * nx * hz + b * hz, hz)].reshape(band, 128)
        return jnp.dot(rows, grad[...], preferred_element_type=F32)

    for h in range(2):

        def core_out(b, _, h=h):
            result = product(1 - core, h, b).astype(BF)
            for c in range(ny):
                other[h, b, c] = result[:, c * 128 : (c + 1) * 128]
            return 0

        lax.fori_loop(0, nx, core_out, 0)
        send(other.at[h], other_in.at[h], 9 + h, dom_at(y, 1 - core))

    drain(other_in.at[0], sem_in.at[9])

    def y_first(b, _):
        result = product(core, 0, b)
        for c in range(ny):
            summed = result[:, c * 128 : (c + 1) * 128] + other_in[0, b, c].astype(F32)
            part_a[c, b] = summed.astype(BF)

            @pl.when(c == y)
            def _():
                kept_a[b] = summed

        return 0

    lax.fori_loop(0, nx, y_first, 0)
    for i in range(1, ny):
        c = (y + i) % ny
        send(part_a.at[c], part_a_in.at[y], 11, dom_at(c, core))

    drain(other_in.at[1], sem_in.at[10])

    def x_first(b, _):
        result = product(core, 1, b)
        for c in range(ny):
            summed = result[:, c * 128 : (c + 1) * 128] + other_in[1, b, c].astype(F32)
            part_b[b, c] = summed.astype(BF)

            @pl.when(b == x)
            def _():
                kept_b[c] = summed

        return 0

    lax.fori_loop(0, nx, x_first, 0)
    for i in range(1, nx):
        b = (x + i) % nx
        send(part_b.at[b], part_b_in.at[x], 12, feat_at(b, z))

    def y_sum(b):
        total = kept_a[b]
        for j in range(1, ny):
            total = total + part_a_in[(y + j) % ny, b].astype(F32)
        return total

    def x_sum(c):
        total = kept_b[c]
        for j in range(1, nx):
            total = total + part_b_in[(x + j) % nx, c].astype(F32)
        return total

    drain(part_a_in.at[pl.ds(0, ny - 1)], sem_in.at[11])

    def x_then(i, _):
        b = (x + i) % nx
        col_a[b] = y_sum(b).astype(BF)
        send(col_a.at[b], col_a_in.at[x], 13, feat_at(b, z))
        return 0

    lax.fori_loop(1, nx, x_then, 0)
    fin[0] = y_sum(x)

    drain(part_b_in.at[pl.ds(0, nx - 1)], sem_in.at[12])

    def y_then(i, _):
        c = (y + i) % ny
        col_b[c] = x_sum(c).astype(BF)
        send(col_b.at[c], col_b_in.at[y], 14, dom_at(c, core))
        return 0

    lax.fori_loop(1, ny, y_then, 0)
    fin[1] = x_sum(y)

    def z_out(i, _):
        peer = i

        @pl.when(peer != z)
        def _():
            send(cell.at[peer], cell_in.at[z], 15, feat_at(x, peer))

        return 0

    drain(col_a_in.at[pl.ds(0, nx - 1)], sem_in.at[13])
    total = fin[0]
    for j in range(1, nx):
        total = total + col_a_in[(x + j) % nx].astype(F32)
    fin[0] = total
    cell[0:hz] = total.astype(BF).reshape(hz, width, 128)
    lax.fori_loop(0, hz, z_out, 0)
    drain(col_b_in.at[pl.ds(0, ny - 1)], sem_in.at[14])
    total = fin[1]
    for j in range(1, ny):
        total = total + col_b_in[(y + j) % ny].astype(F32)
    fin[1] = total
    cell[hz:nz] = total.astype(BF).reshape(hz, width, 128)
    lax.fori_loop(hz, nz, z_out, 0)
    drain(cell_in.at[pl.ds(0, nz - 1)], sem_in.at[15])
    total = fin[half, pl.ds(pl.multiple_of(zz * width, width), width)]
    for j in range(1, nz):
        total = total + cell_in[(z + j) % nz].astype(F32)

    final[dom] = total

    def dom_out(i, _):
        send(final.at[dom], final.at[dom], 16, {"feat": feat, "dom": (dom + i) % nd})
        return 0

    lax.fori_loop(1, nd, dom_out, 0)
    drain(final.at[pl.ds(0, nd - 1)], sem_in.at[16])
    for b in range(ny):
        span = slice(b * 128, (b + 1) * 128)
        gs_ref[:, span] = final[b * nc]
        gn_ref[:, span] = final[b * nc + 1]

    sent = (
        halo_out.at[pl.ds(0, nd - 1)], ext.at[pl.ds(0, nz - 1)], ext.at[pl.ds(0, nf - 1)],
        mean.at[pl.ds(0, nf - 1)], weights.at[0, core, y, pl.ds(0, nx - 1)],
        weights.at[1, core, pl.ds(0, ny - 1), x], weights.at[0, core, pl.ds(0, ny - 1)],
        weights.at[1, core, :, pl.ds(0, nx - 1)], weights.at[0], other.at[0], other.at[1],
        part_a.at[pl.ds(0, ny - 1)], part_b.at[pl.ds(0, nx - 1)],
        col_a.at[pl.ds(0, nx - 1)], col_b.at[pl.ds(0, ny - 1)], cell.at[pl.ds(0, nz - 1)],
        final.at[pl.ds(0, nd - 1)],
    )
    for phase, ref in enumerate(sent):
        drain(ref, sem_out.at[phase])


def on_device(features, w1, w2, cotangent, send_rows, send_count, tile_source, tile_kind, patterns):
    nx, nz = FEAT_GRID
    ny, nc = DOM_GRID
    nf, nd, hz = nx * nz, ny * nc, nz // 2
    width = features.shape[1]
    hidden = w1.shape[1]
    slot_tiles = send_rows.shape[2] // 128
    assert features.shape[0] == nf * 128 and hidden == ny * 128 and nc == 2
    band = hz * width
    vmem = pl.BlockSpec(memory_space=pltpu.VMEM)
    hbm = pl.BlockSpec(memory_space=pltpu.HBM)
    source, kind = tile_source[0].T, tile_kind[0].T
    shapes = (
        jax.ShapeDtypeStruct((128, hidden), BF),
        jax.ShapeDtypeStruct((width, hidden), F32),
        jax.ShapeDtypeStruct((width, hidden), F32),
    )
    return pl.pallas_call(
        layer,
        out_shape=shapes,
        in_specs=[hbm] * 9,
        out_specs=(vmem,) * 3,
        scratch_shapes=[
            pltpu.VMEM((width, nf * 128), BF),
            pltpu.VMEM(send_rows.shape[1:], jnp.int32),
            pltpu.VMEM(patterns.shape, BF),
            pltpu.VMEM((128, hidden), BF),
            pltpu.SMEM(send_count.shape, jnp.int32),
            pltpu.SMEM(source.shape, jnp.int32),
            pltpu.SMEM(kind.shape, jnp.int32),
            pltpu.VMEM((nf + nd * slot_tiles, width, 128), BF),
            pltpu.VMEM((nd, slot_tiles, width, 128), BF),
            pltpu.VMEM((nf, width, 128), BF),
            pltpu.VMEM((2, nf, width, 128), BF),
            pltpu.VMEM((2, nc, ny, nx, hz, width, 128), BF),
            pltpu.VMEM((128, hidden), F32),
            pltpu.VMEM((128, hidden), BF),
            pltpu.VMEM((2, nx, ny, band, 128), BF),
            pltpu.VMEM((2, nx, ny, band, 128), BF),
            pltpu.VMEM((ny, nx, band, 128), BF),
            pltpu.VMEM((ny, nx, band, 128), BF),
            pltpu.VMEM((nx, ny, band, 128), BF),
            pltpu.VMEM((nx, ny, band, 128), BF),
            pltpu.VMEM((nx, band, 128), F32),
            pltpu.VMEM((ny, band, 128), F32),
            pltpu.VMEM((nx, band, 128), BF),
            pltpu.VMEM((nx, band, 128), BF),
            pltpu.VMEM((ny, band, 128), BF),
            pltpu.VMEM((ny, band, 128), BF),
            pltpu.VMEM((2, band, 128), F32),
            pltpu.VMEM((nz, width, 128), BF),
            pltpu.VMEM((nz, width, 128), BF),
            pltpu.VMEM((nd, width, 128), F32),
            pltpu.SemaphoreType.DMA((17,)),
            pltpu.SemaphoreType.DMA((17,)),
            pltpu.SemaphoreType.DMA((8,)),
        ],
        compiler_params=pltpu.CompilerParams(
            collective_id=0, has_side_effects=True, vmem_limit_bytes=67_000_000
        ),
    )(
        features.T, w1, w2, cotangent, send_rows, patterns, send_count, source, kind,
    )


def solution(mesh):
    placed = (
        P("dom", "feat"),
        P("feat", None),
        P("feat", None),
        P(("dom", "feat"), None),
        P(),
        P(),
        P("dom", None, None),
        P("dom", None, None),
        P(),
    )
    return jax.shard_map(
        on_device,
        mesh=mesh,
        in_specs=placed,
        out_specs=(P(("dom", "feat"), None), P("feat", None), P("feat", None)),
        check_vma=False,
    )
```

```python
import jax
import jax.numpy as jnp
from jax import lax
from jax.experimental import pallas as pl
from jax.experimental.pallas import tpu as pltpu
from jax.sharding import PartitionSpec as P

FEAT_GRID = (4, 16)
DOM_GRID = (4, 2)
inv_root_two = 0.7071067811865476
inv_root_two_pi = 0.3989422804014327
BF = jnp.bfloat16
F32 = jnp.float32
MESH = pl.DeviceIdType.MESH


def gelu_pair(linear):
    normal_cdf = 0.5 * (1.0 + lax.erf(linear * inv_root_two))
    density = jnp.exp(-0.5 * linear * linear) * inv_root_two_pi
    return linear * normal_cdf, normal_cdf + linear * density


def drain(ref, sem):
    pltpu.make_async_copy(ref, ref, sem).wait()


def layer(
    x_hbm, w1_hbm, w2_hbm, cot_hbm, rows_hbm, pat_hbm, count_hbm, source_hbm, kind_hbm,
    hid_ref, gs_ref, gn_ref,
    x_own, wanted_ref, pats, cot, count_ref, source_ref, kind_ref,
    ext, halo_out, mean, xm, weights, partial, grad, other_a, other_a_in, other_b, other_b_in,
    part_a, part_a_in, part_b, part_b_in, kept_a, kept_b,
    col_a, col_a_in, col_b, col_b_in, fin, cell, cell_in, final,
    sem_out, sem_in, load_sem,
):
    nx, nz = FEAT_GRID
    ny, nc = DOM_GRID
    nf, nd, hz = nx * nz, ny * nc, nz // 2
    feat = lax.axis_index("feat")
    dom = lax.axis_index("dom")
    x, z = feat // nz, feat % nz
    y, core = dom // nc, dom % nc
    half, zz = z // hz, z % hz
    slot = half * (nx * hz) + x * hz + zz
    width = x_own.shape[0]
    depth = nx * hz * width
    band = hz * width
    tiles = nf
    slot_tiles = halo_out.shape[1]
    slots = wanted_ref.shape[1]
    steps = source_ref.shape[0]

    def send(src, dst, phase, where):
        pltpu.make_async_remote_copy(
            src_ref=src, dst_ref=dst, send_sem=sem_out.at[phase], recv_sem=sem_in.at[phase],
            device_id=where, device_id_type=MESH,
        ).start()

    def feat_at(fx, fz):
        return {"feat": fx * nz + fz, "dom": dom}

    def dom_at(dy, dc):
        return {"feat": feat, "dom": dy * nc + dc}

    block = pl.ds(pl.multiple_of(y * 128, 128), 128)
    my_unit = weights.at[half, core, y, x, zz]
    loads = [
        pltpu.make_async_copy(src, dst, load_sem.at[i])
        for i, (src, dst) in enumerate((
            (x_hbm, x_own), (rows_hbm.at[dom], wanted_ref), (count_hbm, count_ref),
            (pat_hbm, pats), (source_hbm, source_ref), (kind_hbm, kind_ref), (cot_hbm, cot),
        ))
    ]
    barrier = pltpu.get_barrier_semaphore()

    def greet_feat(i, _):
        pl.semaphore_signal(
            barrier, inc=1, device_id={"feat": (feat + far + i) % nf, "dom": dom}, device_id_type=MESH
        )
        return 0

    def greet_dom(i, _):
        pl.semaphore_signal(
            barrier, inc=1, device_id={"feat": feat, "dom": (dom + i) % nd}, device_id_type=MESH
        )
        return 0

    far = hz
    lax.fori_loop(0, nf - hz, greet_feat, 0)
    lax.fori_loop(nf - hz + 1, nf, greet_feat, 0)
    lax.fori_loop(1, nd, greet_dom, 0)
    for load in loads:
        load.start()

    @pl.when(core == 0)
    def _():
        pltpu.make_async_copy(w1_hbm.at[:, block], my_unit, load_sem.at[7]).start()

    @pl.when(core == 1)
    def _():
        pltpu.make_async_copy(w2_hbm.at[:, block], my_unit, load_sem.at[7]).start()

    for load in loads[:3]:
        load.wait()

    def take(t, _):
        ext[t] = x_own[:, pl.ds(pl.multiple_of(t * 128, 128), 128)]
        return 0

    lax.fori_loop(0, tiles, take, 0)
    xm[0, slot] = ext[feat]

    group = min(tiles, 16)
    lane_ids = lax.broadcasted_iota(jnp.int32, (128, slots), 0)
    slot_ids = lax.broadcasted_iota(jnp.int32, (1, slots), 1)

    def pick(dest, _):
        wanted = wanted_ref[pl.ds(dest, 1), :]
        low, high = wanted & 127, wanted >> 7
        choose = jnp.where(lane_ids == low, 1.0, 0.0).astype(BF)
        found = jnp.zeros((width, slots), F32)
        for g in range(0, tiles, group):
            rows = ext[g : g + group].reshape(group * width, 128)
            spread = jnp.dot(rows, choose, preferred_element_type=F32)
            for h in range(group):
                found = jnp.where(
                    high == g + h, spread[h * width : (h + 1) * width], found
                )
        live = slot_ids < count_ref[dom, dest]
        found = jnp.where(live, found, 0.0).astype(BF)
        for j in range(slot_tiles):
            halo_out[dest, j] = found[:, j * 128 : (j + 1) * 128]
        return 0

    lax.fori_loop(0, nd, pick, 0)
    halo_at = tiles + dom * slot_tiles
    for j in range(slot_tiles):
        ext[halo_at + j] = halo_out[dom, j]
    pltpu.make_async_copy(my_unit, my_unit, load_sem.at[7]).wait()
    for load in loads[3:]:
        load.wait()
    pl.semaphore_wait(barrier, nf - 1 + nd - 1)

    def halo_send(i, _):
        dest = (dom + i) % nd
        send(
            halo_out.at[dest], ext.at[pl.ds(halo_at, slot_tiles)], 0,
            {"feat": feat, "dom": dest},
        )
        return 0

    lax.fori_loop(1, nd, halo_send, 0)

    def weights_z(i, _):
        send(my_unit, my_unit, 1, feat_at(x, (z + i) % nz))
        return 0

    lax.fori_loop(1, nz, weights_z, 0)

    def features_out(i, _):
        peer = (feat + i) % nf
        send(ext.at[peer], xm.at[0, slot], 2, {"feat": peer, "dom": dom})
        return 0

    lax.fori_loop(1, nf, features_out, 0)

    ones = jnp.ones((width, 256), BF)

    def mean_of(t):
        total = jnp.zeros((2 * width, 128), F32)
        for k in range(0, steps, 2):
            left = jnp.concatenate([ext[source_ref[k, t]], ext[source_ref[k + 1, t]]], axis=1)
            right = jnp.concatenate([pats[kind_ref[k, t]], pats[kind_ref[k + 1, t]]], axis=1)
            total = total + lax.dot_general(
                jnp.concatenate([left, ones], axis=0), right, (((1,), (1,)), ((), ())),
                preferred_element_type=F32,
            )
        return (total[:width] / total[width : width + 1]).astype(BF)

    def mean_out(i, _):
        peers = [(feat + 1 + 2 * i + j) % nf for j in range(2)]
        found = [mean_of(peer) for peer in peers]
        for peer, value in zip(peers, found):
            mean[peer] = value
        for peer in peers:

            @pl.when(peer != feat)
            def _():
                send(mean.at[peer], xm.at[1, slot], 3, {"feat": peer, "dom": dom})

        return 0

    drain(ext.at[pl.ds(tiles, (nd - 1) * slot_tiles)], sem_in.at[0])
    lax.fori_loop(0, nf // 2, mean_out, 0)
    xm[1, slot] = mean[feat]

    drain(ext.at[pl.ds(0, nz - 1)], sem_in.at[1])
    first_a, first_b = weights.at[0, core, y, x], weights.at[1, core, y, x]
    for i in range(1, nx):
        send(first_a, first_a, 4, feat_at((x + i) % nx, z))
    for i in range(1, ny):
        send(first_b, first_b, 5, dom_at((y + i) % ny, core))
    drain(weights.at[0, core, y, pl.ds(0, nx - 1)], sem_in.at[4])
    then_a = weights.at[0, core, y]
    for i in range(1, ny):
        send(then_a, then_a, 6, dom_at((y + i) % ny, core))
    drain(weights.at[1, core, pl.ds(0, ny - 1), x], sem_in.at[5])
    then_b = weights.at[1, core, :, x]
    for i in range(1, nx):
        send(then_b, then_b, 7, feat_at((x + i) % nx, z))
    drain(weights.at[0, core, pl.ds(0, ny - 1)], sem_in.at[6])
    drain(weights.at[1, core, :, pl.ds(0, nx - 1)], sem_in.at[7])
    for h in range(2):
        send(weights.at[h, core], weights.at[h, core], 8, dom_at(y, 1 - core))
    drain(xm.at[0, pl.ds(0, nf - 1)], sem_in.at[2])

    def times_weights(m, own, b):
        total = jnp.zeros((128, 128), F32)
        for h in range(2):
            total = total + lax.dot_general(
                own[h], weights[h, m, b].reshape(depth, 128), (((0,), (0,)), ((), ())),
                preferred_element_type=F32,
            )
        return total

    def halves(m):
        return [xm[m, h * nx * hz : (h + 1) * nx * hz].reshape(depth, 128) for h in range(2)]

    drain(weights.at[0], sem_in.at[8])
    own = halves(0)
    for b in range(ny):
        partial[:, b * 128 : (b + 1) * 128] = times_weights(0, own, b)
    drain(xm.at[1, pl.ds(0, nf - 1)], sem_in.at[3])
    own = halves(1)
    for b in range(ny):
        span = slice(b * 128, (b + 1) * 128)
        value, slope = gelu_pair(partial[:, span] + times_weights(1, own, b))
        hid_ref[:, span] = value.astype(BF)
        grad[:, span] = (cot[:, span].astype(F32) * slope).astype(BF)

    def rows_of(m, h, b):
        return xm[m, pl.ds(h * nx * hz + b * hz, hz)].reshape(band, 128)

    def product_a(m, b):
        return jnp.dot(rows_of(m, 0, b), grad[...], preferred_element_type=F32)

    def product_b(m, b, p):
        columns = grad[:, p * cb * 128 : (p + 1) * cb * 128]
        return jnp.dot(rows_of(m, 1, b), columns, preferred_element_type=F32)

    ca, cb = nx // 2, ny // 2
    for p in range(2):

        def core_a(b, _):
            result = product_a(1 - core, b).astype(BF)
            for c in range(ny):
                other_a[b, c] = result[:, c * 128 : (c + 1) * 128]
            return 0

        def core_b(b, _, p=p):
            result = product_b(1 - core, b, p).astype(BF)
            for c in range(cb):
                other_b[p * cb + c, b] = result[:, c * 128 : (c + 1) * 128]
            return 0

        lax.fori_loop(p * ca, (p + 1) * ca, core_a, 0)
        piece = pl.ds(p * ca, ca)
        send(other_a.at[piece], other_a_in.at[piece], 9 + p, dom_at(y, 1 - core))
        lax.fori_loop(0, nx, core_b, 0)
        piece = pl.ds(p * cb, cb)
        send(other_b.at[piece], other_b_in.at[piece], 11 + p, dom_at(y, 1 - core))

    for p in range(2):

        def y_first(b, _):
            result = product_a(core, b)
            for c in range(ny):
                summed = result[:, c * 128 : (c + 1) * 128] + other_a_in[b, c].astype(F32)
                part_a[c, b] = summed.astype(BF)

                @pl.when(c == y)
                def _():
                    kept_a[b] = summed

            return 0

        def x_first(b, _, p=p):
            result = product_b(core, b, p)
            for c in range(cb):
                column = p * cb + c
                summed = result[:, c * 128 : (c + 1) * 128] + other_b_in[column, b].astype(F32)
                part_b[b, column] = summed.astype(BF)

                @pl.when(b == x)
                def _():
                    kept_b[column] = summed

            return 0

        piece = pl.ds(p * ca, ca)
        drain(other_a_in.at[piece], sem_in.at[9 + p])
        lax.fori_loop(p * ca, (p + 1) * ca, y_first, 0)
        for i in range(1, ny):
            c = (y + i) % ny
            send(part_a.at[c, piece], part_a_in.at[y, piece], 13, dom_at(c, core))
        piece = pl.ds(p * cb, cb)
        drain(other_b_in.at[piece], sem_in.at[11 + p])
        lax.fori_loop(0, nx, x_first, 0)
        for i in range(1, nx):
            b = (x + i) % nx
            send(part_b.at[b, piece], part_b_in.at[x, piece], 14, feat_at(b, z))

    def y_sum(b):
        total = kept_a[b]
        for j in range(1, ny):
            total = total + part_a_in[(y + j) % ny, b].astype(F32)
        return total

    def x_sum(c):
        total = kept_b[c]
        for j in range(1, nx):
            total = total + part_b_in[(x + j) % nx, c].astype(F32)
        return total

    drain(part_a_in.at[pl.ds(0, ny - 1)], sem_in.at[13])

    def x_then(i, _):
        b = (x + i) % nx
        col_a[b] = y_sum(b).astype(BF)
        send(col_a.at[b], col_a_in.at[x], 15, feat_at(b, z))
        return 0

    lax.fori_loop(1, nx, x_then, 0)
    fin[0] = y_sum(x)

    drain(part_b_in.at[pl.ds(0, nx - 1)], sem_in.at[14])

    def y_then(i, _):
        c = (y + i) % ny
        col_b[c] = x_sum(c).astype(BF)
        send(col_b.at[c], col_b_in.at[y], 16, dom_at(c, core))
        return 0

    lax.fori_loop(1, ny, y_then, 0)
    fin[1] = x_sum(y)

    def z_out(i, _):
        peer = i

        @pl.when(peer != z)
        def _():
            send(cell.at[peer], cell_in.at[z], 17, feat_at(x, peer))

        return 0

    drain(col_a_in.at[pl.ds(0, nx - 1)], sem_in.at[15])
    total = fin[0]
    for j in range(1, nx):
        total = total + col_a_in[(x + j) % nx].astype(F32)
    fin[0] = total
    cell[0:hz] = total.astype(BF).reshape(hz, width, 128)
    lax.fori_loop(0, hz, z_out, 0)
    drain(col_b_in.at[pl.ds(0, ny - 1)], sem_in.at[16])
    total = fin[1]
    for j in range(1, ny):
        total = total + col_b_in[(y + j) % ny].astype(F32)
    fin[1] = total
    cell[hz:nz] = total.astype(BF).reshape(hz, width, 128)
    lax.fori_loop(hz, nz, z_out, 0)
    drain(cell_in.at[pl.ds(0, nz - 1)], sem_in.at[17])
    total = fin[half, pl.ds(pl.multiple_of(zz * width, width), width)]
    for j in range(1, nz):
        total = total + cell_in[(z + j) % nz].astype(F32)

    final[dom] = total

    def dom_out(i, _):
        send(final.at[dom], final.at[dom], 18, {"feat": feat, "dom": (dom + i) % nd})
        return 0

    lax.fori_loop(1, nd, dom_out, 0)
    drain(final.at[pl.ds(0, nd - 1)], sem_in.at[18])
    for b in range(ny):
        span = slice(b * 128, (b + 1) * 128)
        gs_ref[:, span] = final[b * nc]
        gn_ref[:, span] = final[b * nc + 1]

    sent = (
        halo_out.at[pl.ds(0, nd - 1)], ext.at[pl.ds(0, nz - 1)], ext.at[pl.ds(0, nf - 1)],
        mean.at[pl.ds(0, nf - 1)], weights.at[0, core, y, pl.ds(0, nx - 1)],
        weights.at[1, core, pl.ds(0, ny - 1), x], weights.at[0, core, pl.ds(0, ny - 1)],
        weights.at[1, core, :, pl.ds(0, nx - 1)], weights.at[0],
        other_a.at[pl.ds(0, nx // 2)], other_a.at[pl.ds(0, nx // 2)],
        other_b.at[pl.ds(0, ny // 2)], other_b.at[pl.ds(0, ny // 2)],
        part_a.at[pl.ds(0, ny - 1)], part_b.at[pl.ds(0, nx - 1)],
        col_a.at[pl.ds(0, nx - 1)], col_b.at[pl.ds(0, ny - 1)], cell.at[pl.ds(0, nz - 1)],
        final.at[pl.ds(0, nd - 1)],
    )
    for phase, ref in enumerate(sent):
        drain(ref, sem_out.at[phase])


def store_out(hid_in, gs_in, gn_in, hid_ref, gs_ref, gn_ref, hid_buf, gs_buf, gn_buf, sems):
    bufs = (hid_buf, gs_buf, gn_buf)
    ins = [
        pltpu.make_async_copy(a, b, sems.at[i])
        for i, (a, b) in enumerate(zip((hid_in, gs_in, gn_in), bufs))
    ]
    outs = [
        pltpu.make_async_copy(a, b, sems.at[3 + i])
        for i, (a, b) in enumerate(zip(bufs, (hid_ref, gs_ref, gn_ref)))
    ]
    for copy in ins:
        copy.start()
    for i in range(3):
        ins[i].wait()
        outs[i].start()
    for copy in outs:
        copy.wait()


def on_device(features, w1, w2, cotangent, send_rows, send_count, tile_source, tile_kind, patterns):
    nx, nz = FEAT_GRID
    ny, nc = DOM_GRID
    nf, nd, hz = nx * nz, ny * nc, nz // 2
    width = features.shape[1]
    hidden = w1.shape[1]
    slot_tiles = send_rows.shape[2] // 128
    assert features.shape[0] == nf * 128 and hidden == ny * 128 and nc == 2
    band = hz * width
    vmem = pl.BlockSpec(memory_space=pltpu.VMEM)
    hbm = pl.BlockSpec(memory_space=pltpu.HBM)
    source, kind = tile_source[0].T, tile_kind[0].T
    shapes = (
        jax.ShapeDtypeStruct((128, hidden), BF),
        jax.ShapeDtypeStruct((width, hidden), F32),
        jax.ShapeDtypeStruct((width, hidden), F32),
    )
    results = pl.pallas_call(
        layer,
        out_shape=shapes,
        in_specs=[hbm] * 9,
        out_specs=(vmem,) * 3,
        scratch_shapes=[
            pltpu.VMEM((width, nf * 128), BF),
            pltpu.VMEM(send_rows.shape[1:], jnp.int32),
            pltpu.VMEM(patterns.shape, BF),
            pltpu.VMEM((128, hidden), BF),
            pltpu.SMEM(send_count.shape, jnp.int32),
            pltpu.SMEM(source.shape, jnp.int32),
            pltpu.SMEM(kind.shape, jnp.int32),
            pltpu.VMEM((nf + nd * slot_tiles, width, 128), BF),
            pltpu.VMEM((nd, slot_tiles, width, 128), BF),
            pltpu.VMEM((nf, width, 128), BF),
            pltpu.VMEM((2, nf, width, 128), BF),
            pltpu.VMEM((2, nc, ny, nx, hz, width, 128), BF),
            pltpu.VMEM((128, hidden), F32),
            pltpu.VMEM((128, hidden), BF),
            pltpu.VMEM((nx, ny, band, 128), BF),
            pltpu.VMEM((nx, ny, band, 128), BF),
            pltpu.VMEM((ny, nx, band, 128), BF),
            pltpu.VMEM((ny, nx, band, 128), BF),
            pltpu.VMEM((ny, nx, band, 128), BF),
            pltpu.VMEM((ny, nx, band, 128), BF),
            pltpu.VMEM((nx, ny, band, 128), BF),
            pltpu.VMEM((nx, ny, band, 128), BF),
            pltpu.VMEM((nx, band, 128), F32),
            pltpu.VMEM((ny, band, 128), F32),
            pltpu.VMEM((nx, band, 128), BF),
            pltpu.VMEM((nx, band, 128), BF),
            pltpu.VMEM((ny, band, 128), BF),
            pltpu.VMEM((ny, band, 128), BF),
            pltpu.VMEM((2, band, 128), F32),
            pltpu.VMEM((nz, width, 128), BF),
            pltpu.VMEM((nz, width, 128), BF),
            pltpu.VMEM((nd, width, 128), F32),
            pltpu.SemaphoreType.DMA((19,)),
            pltpu.SemaphoreType.DMA((19,)),
            pltpu.SemaphoreType.DMA((8,)),
        ],
        compiler_params=pltpu.CompilerParams(
            collective_id=0, has_side_effects=True, vmem_limit_bytes=67_000_000
        ),
    )(
        features.T, w1, w2, cotangent, send_rows, patterns, send_count, source, kind,
    )
    return pl.pallas_call(
        store_out,
        out_shape=shapes,
        in_specs=[hbm] * 3,
        out_specs=(hbm,) * 3,
        scratch_shapes=[pltpu.VMEM(a.shape, a.dtype) for a in shapes]
        + [pltpu.SemaphoreType.DMA((6,))],
        compiler_params=pltpu.CompilerParams(vmem_limit_bytes=67_000_000),
    )(*results)


def solution(mesh):
    placed = (
        P("dom", "feat"),
        P("feat", None),
        P("feat", None),
        P(("dom", "feat"), None),
        P(),
        P(),
        P("dom", None, None),
        P("dom", None, None),
        P(),
    )
    return jax.shard_map(
        on_device,
        mesh=mesh,
        in_specs=placed,
        out_specs=(P(("dom", "feat"), None), P("feat", None), P("feat", None)),
        check_vma=False,
    )
```

```python
import jax
import jax.numpy as jnp
from jax import lax
from jax.experimental import pallas as pl
from jax.experimental.pallas import tpu as pltpu
from jax.sharding import PartitionSpec as P

FEAT_GRID = (4, 16)
DOM_GRID = (4, 2)
inv_root_two = 0.7071067811865476
inv_root_two_pi = 0.3989422804014327
BF = jnp.bfloat16
F32 = jnp.float32
MESH = pl.DeviceIdType.MESH


def gelu_pair(linear):
    normal_cdf = 0.5 * (1.0 + lax.erf(linear * inv_root_two))
    density = jnp.exp(-0.5 * linear * linear) * inv_root_two_pi
    return linear * normal_cdf, normal_cdf + linear * density


def drain(ref, sem):
    pltpu.make_async_copy(ref, ref, sem).wait()


def layer(
    x_hbm, w1_hbm, w2_hbm, cot_hbm, rows_hbm, pat_hbm, count_hbm, source_hbm, kind_hbm,
    hid_ref, gs_ref, gn_ref,
    x_own, wanted_ref, pats, cot, count_ref, source_ref, kind_ref,
    ext, halo_out, mean, xm, weights, partial, grad, other_a, other_a_in, other_b, other_b_in,
    part_a, part_a_in, part_b, part_b_in, kept_a, kept_b,
    col_a, col_a_in, col_b, col_b_in, fin, cell, cell_in, final,
    sem_out, sem_in, load_sem, round_sem,
):
    nx, nz = FEAT_GRID
    ny, nc = DOM_GRID
    nf, nd, hz = nx * nz, ny * nc, nz // 2
    feat = lax.axis_index("feat")
    dom = lax.axis_index("dom")
    x, z = feat // nz, feat % nz
    y, core = dom // nc, dom % nc
    half, zz = z // hz, z % hz
    slot = half * (nx * hz) + x * hz + zz
    width = x_own.shape[0]
    depth = nx * hz * width
    band = hz * width
    tiles = nf
    slot_tiles = halo_out.shape[1]
    slots = wanted_ref.shape[1]
    steps = source_ref.shape[0]

    def send(src, dst, phase, where):
        pltpu.make_async_remote_copy(
            src_ref=src, dst_ref=dst, send_sem=sem_out.at[phase], recv_sem=sem_in.at[phase],
            device_id=where, device_id_type=MESH,
        ).start()

    def feat_at(fx, fz):
        return {"feat": fx * nz + fz, "dom": dom}

    def dom_at(dy, dc):
        return {"feat": feat, "dom": dy * nc + dc}

    block = pl.ds(pl.multiple_of(y * 128, 128), 128)
    my_unit = weights.at[half, core, y, x, zz]
    loads = [
        pltpu.make_async_copy(src, dst, load_sem.at[i])
        for i, (src, dst) in enumerate((
            (x_hbm, x_own), (rows_hbm.at[dom], wanted_ref), (count_hbm, count_ref),
            (pat_hbm, pats), (source_hbm, source_ref), (kind_hbm, kind_ref), (cot_hbm, cot),
        ))
    ]
    barrier = pltpu.get_barrier_semaphore()

    def along(*distances):
        return sorted(({d % nz for d in distances} | {-d % nz for d in distances}) - {0})

    near = along(1, 2)
    for i in near:
        pl.semaphore_signal(barrier, inc=1, device_id=feat_at(x, (z + i) % nz), device_id_type=MESH)
    for i in range(1, nx):
        pl.semaphore_signal(barrier, inc=1, device_id=feat_at((x + i) % nx, z), device_id_type=MESH)
    for i in range(1, nd):
        pl.semaphore_signal(
            barrier, inc=1, device_id={"feat": feat, "dom": (dom + i) % nd}, device_id_type=MESH
        )

    def round_out(r, offsets):
        for i in offsets:
            pl.semaphore_signal(
                round_sem.at[r], inc=1, device_id=feat_at(x, (z + i) % nz), device_id_type=MESH
            )

    for load in loads:
        load.start()

    @pl.when(core == 0)
    def _():
        pltpu.make_async_copy(w1_hbm.at[:, block], my_unit, load_sem.at[7]).start()

    @pl.when(core == 1)
    def _():
        pltpu.make_async_copy(w2_hbm.at[:, block], my_unit, load_sem.at[7]).start()

    for load in loads[:3]:
        load.wait()

    def take(t, _):
        ext[t] = x_own[:, pl.ds(pl.multiple_of(t * 128, 128), 128)]
        return 0

    lax.fori_loop(0, tiles, take, 0)
    xm[0, slot] = ext[feat]

    group = min(tiles, 16)
    lane_ids = lax.broadcasted_iota(jnp.int32, (128, slots), 0)
    slot_ids = lax.broadcasted_iota(jnp.int32, (1, slots), 1)

    halo_at = tiles + dom * slot_tiles

    def pick(i, _):
        dest = (dom + i) % nd
        wanted = wanted_ref[pl.ds(dest, 1), :]
        low, high = wanted & 127, wanted >> 7
        choose = jnp.where(lane_ids == low, 1.0, 0.0).astype(BF)
        found = jnp.zeros((width, slots), F32)
        for g in range(0, tiles, group):
            rows = ext[g : g + group].reshape(group * width, 128)
            spread = jnp.dot(rows, choose, preferred_element_type=F32)
            for h in range(group):
                found = jnp.where(
                    high == g + h, spread[h * width : (h + 1) * width], found
                )
        live = slot_ids < count_ref[dom, dest]
        found = jnp.where(live, found, 0.0).astype(BF)
        for j in range(slot_tiles):
            halo_out[dest, j] = found[:, j * 128 : (j + 1) * 128]

        @pl.when(dest != dom)
        def _():
            send(
                halo_out.at[dest], ext.at[pl.ds(halo_at, slot_tiles)], 0,
                {"feat": feat, "dom": dest},
            )

        return 0

    def outward(first, count):
        def weights_z(i, _):
            there = (z + first + i) % nz

            @pl.when(there != z)
            def _():
                send(my_unit, my_unit, 1, feat_at(x, there))

            return 0

        def features_out(i, _):
            peer = (x + i) % nx * nz + (z + first + i // nx) % nz

            @pl.when(peer != feat)
            def _():
                send(ext.at[peer], xm.at[0, slot], 2, {"feat": peer, "dom": dom})

            return 0

        lax.fori_loop(0, count, weights_z, 0)
        lax.fori_loop(0, count * nx, features_out, 0)

    if nz > 11:
        reach = (((nz - 2, 5),), ((3, 3), (nz - 5, 3)), ((6, nz - 11),))
    elif nz > 5:
        reach = (((nz - 2, 5),), ((3, nz - 5),), ())
    else:
        reach = (((0, nz),), (), ())
    third = nd // 3 + 1
    pl.semaphore_wait(barrier, len(near) + nx - 1 + nd - 1)
    for r, offsets in enumerate((near, along(3), along(5))):
        round_out(r, offsets)
        lax.fori_loop(r * third, min((r + 1) * third, nd), pick, 0)
        if r == 0:
            pltpu.make_async_copy(my_unit, my_unit, load_sem.at[7]).wait()
            for load in loads[3:]:
                load.wait()
        pl.semaphore_wait(round_sem.at[r], len(offsets))
        for first, count in reach[r]:
            outward(first, count)
    for j in range(slot_tiles):
        ext[halo_at + j] = halo_out[dom, j]

    ones = jnp.ones((width, 256), BF)

    def mean_of(t):
        total = jnp.zeros((2 * width, 128), F32)
        for k in range(0, steps, 2):
            left = jnp.concatenate([ext[source_ref[k, t]], ext[source_ref[k + 1, t]]], axis=1)
            right = jnp.concatenate([pats[kind_ref[k, t]], pats[kind_ref[k + 1, t]]], axis=1)
            total = total + lax.dot_general(
                jnp.concatenate([left, ones], axis=0), right, (((1,), (1,)), ((), ())),
                preferred_element_type=F32,
            )
        return (total[:width] / total[width : width + 1]).astype(BF)

    def mean_out(i, _):
        peers = [(feat + 1 + 2 * i + j) % nf for j in range(2)]
        found = [mean_of(peer) for peer in peers]
        for peer, value in zip(peers, found):
            mean[peer] = value
        for peer in peers:

            @pl.when(peer != feat)
            def _():
                send(mean.at[peer], xm.at[1, slot], 3, {"feat": peer, "dom": dom})

        return 0

    drain(ext.at[pl.ds(tiles, (nd - 1) * slot_tiles)], sem_in.at[0])
    lax.fori_loop(0, nf // 2, mean_out, 0)
    xm[1, slot] = mean[feat]

    drain(ext.at[pl.ds(0, nz - 1)], sem_in.at[1])
    first_a, first_b = weights.at[0, core, y, x], weights.at[1, core, y, x]
    for i in range(1, nx):
        send(first_a, first_a, 4, feat_at((x + i) % nx, z))
    for i in range(1, ny):
        send(first_b, first_b, 5, dom_at((y + i) % ny, core))
    drain(weights.at[0, core, y, pl.ds(0, nx - 1)], sem_in.at[4])
    then_a = weights.at[0, core, y]
    for i in range(1, ny):
        send(then_a, then_a, 6, dom_at((y + i) % ny, core))
    drain(weights.at[1, core, pl.ds(0, ny - 1), x], sem_in.at[5])
    then_b = weights.at[1, core, :, x]
    for i in range(1, nx):
        send(then_b, then_b, 7, feat_at((x + i) % nx, z))
    drain(weights.at[0, core, pl.ds(0, ny - 1)], sem_in.at[6])
    drain(weights.at[1, core, :, pl.ds(0, nx - 1)], sem_in.at[7])
    for h in range(2):
        send(weights.at[h, core], weights.at[h, core], 8, dom_at(y, 1 - core))
    drain(xm.at[0, pl.ds(0, nf - 1)], sem_in.at[2])

    def times_weights(m, own, b):
        total = jnp.zeros((128, 128), F32)
        for h in range(2):
            total = total + lax.dot_general(
                own[h], weights[h, m, b].reshape(depth, 128), (((0,), (0,)), ((), ())),
                preferred_element_type=F32,
            )
        return total

    def halves(m):
        return [xm[m, h * nx * hz : (h + 1) * nx * hz].reshape(depth, 128) for h in range(2)]

    drain(weights.at[0], sem_in.at[8])
    own = halves(0)
    for b in range(ny):
        partial[:, b * 128 : (b + 1) * 128] = times_weights(0, own, b)
    drain(xm.at[1, pl.ds(0, nf - 1)], sem_in.at[3])
    own = halves(1)
    for b in range(ny):
        span = slice(b * 128, (b + 1) * 128)
        value, slope = gelu_pair(partial[:, span] + times_weights(1, own, b))
        hid_ref[:, span] = value.astype(BF)
        grad[:, span] = (cot[:, span].astype(F32) * slope).astype(BF)

    def rows_of(m, h, b):
        return xm[m, pl.ds(h * nx * hz + b * hz, hz)].reshape(band, 128)

    def product_a(m, b):
        return jnp.dot(rows_of(m, 0, b), grad[...], preferred_element_type=F32)

    def product_b(m, b, p):
        columns = grad[:, p * cb * 128 : (p + 1) * cb * 128]
        return jnp.dot(rows_of(m, 1, b), columns, preferred_element_type=F32)

    ca, cb = nx // 2, ny // 2
    for p in range(2):

        def core_a(b, _):
            result = product_a(1 - core, b).astype(BF)
            for c in range(ny):
                other_a[b, c] = result[:, c * 128 : (c + 1) * 128]
            return 0

        def core_b(b, _, p=p):
            result = product_b(1 - core, b, p).astype(BF)
            for c in range(cb):
                other_b[p * cb + c, b] = result[:, c * 128 : (c + 1) * 128]
            return 0

        lax.fori_loop(p * ca, (p + 1) * ca, core_a, 0)
        piece = pl.ds(p * ca, ca)
        send(other_a.at[piece], other_a_in.at[piece], 9 + p, dom_at(y, 1 - core))
        lax.fori_loop(0, nx, core_b, 0)
        piece = pl.ds(p * cb, cb)
        send(other_b.at[piece], other_b_in.at[piece], 11 + p, dom_at(y, 1 - core))

    for p in range(2):

        def y_first(b, _):
            result = product_a(core, b)
            for c in range(ny):
                summed = result[:, c * 128 : (c + 1) * 128] + other_a_in[b, c].astype(F32)
                part_a[c, b] = summed.astype(BF)

                @pl.when(c == y)
                def _():
                    kept_a[b] = summed

            return 0

        def x_first(b, _, p=p):
            result = product_b(core, b, p)
            for c in range(cb):
                column = p * cb + c
                summed = result[:, c * 128 : (c + 1) * 128] + other_b_in[column, b].astype(F32)
                part_b[b, column] = summed.astype(BF)

                @pl.when(b == x)
                def _():
                    kept_b[column] = summed

            return 0

        piece = pl.ds(p * ca, ca)
        drain(other_a_in.at[piece], sem_in.at[9 + p])
        lax.fori_loop(p * ca, (p + 1) * ca, y_first, 0)
        for i in range(1, ny):
            c = (y + i) % ny
            send(part_a.at[c, piece], part_a_in.at[y, piece], 13, dom_at(c, core))
        piece = pl.ds(p * cb, cb)
        drain(other_b_in.at[piece], sem_in.at[11 + p])
        lax.fori_loop(0, nx, x_first, 0)
        for i in range(1, nx):
            b = (x + i) % nx
            send(part_b.at[b, piece], part_b_in.at[x, piece], 14, feat_at(b, z))

    def y_sum(b):
        total = kept_a[b]
        for j in range(1, ny):
            total = total + part_a_in[(y + j) % ny, b].astype(F32)
        return total

    def x_sum(c):
        total = kept_b[c]
        for j in range(1, nx):
            total = total + part_b_in[(x + j) % nx, c].astype(F32)
        return total

    drain(part_a_in.at[pl.ds(0, ny - 1)], sem_in.at[13])

    def x_then(i, _):
        b = (x + i) % nx
        col_a[b] = y_sum(b).astype(BF)
        send(col_a.at[b], col_a_in.at[x], 15, feat_at(b, z))
        return 0

    lax.fori_loop(1, nx, x_then, 0)
    fin[0] = y_sum(x)

    drain(part_b_in.at[pl.ds(0, nx - 1)], sem_in.at[14])

    def y_then(i, _):
        c = (y + i) % ny
        col_b[c] = x_sum(c).astype(BF)
        send(col_b.at[c], col_b_in.at[y], 16, dom_at(c, core))
        return 0

    lax.fori_loop(1, ny, y_then, 0)
    fin[1] = x_sum(y)

    def z_out(i, _):
        peer = i

        @pl.when(peer != z)
        def _():
            send(cell.at[peer], cell_in.at[z], 17, feat_at(x, peer))

        return 0

    drain(col_a_in.at[pl.ds(0, nx - 1)], sem_in.at[15])
    total = fin[0]
    for j in range(1, nx):
        total = total + col_a_in[(x + j) % nx].astype(F32)
    fin[0] = total
    cell[0:hz] = total.astype(BF).reshape(hz, width, 128)
    lax.fori_loop(0, hz, z_out, 0)
    drain(col_b_in.at[pl.ds(0, ny - 1)], sem_in.at[16])
    total = fin[1]
    for j in range(1, ny):
        total = total + col_b_in[(y + j) % ny].astype(F32)
    fin[1] = total
    cell[hz:nz] = total.astype(BF).reshape(hz, width, 128)
    lax.fori_loop(hz, nz, z_out, 0)
    drain(cell_in.at[pl.ds(0, nz - 1)], sem_in.at[17])
    total = fin[half, pl.ds(pl.multiple_of(zz * width, width), width)]
    for j in range(1, nz):
        total = total + cell_in[(z + j) % nz].astype(F32)

    final[dom] = total

    def dom_out(i, _):
        send(final.at[dom], final.at[dom], 18, {"feat": feat, "dom": (dom + i) % nd})
        return 0

    lax.fori_loop(1, nd, dom_out, 0)
    drain(final.at[pl.ds(0, nd - 1)], sem_in.at[18])
    for b in range(ny):
        span = slice(b * 128, (b + 1) * 128)
        gs_ref[:, span] = final[b * nc]
        gn_ref[:, span] = final[b * nc + 1]

    sent = (
        halo_out.at[pl.ds(0, nd - 1)], ext.at[pl.ds(0, nz - 1)], ext.at[pl.ds(0, nf - 1)],
        mean.at[pl.ds(0, nf - 1)], weights.at[0, core, y, pl.ds(0, nx - 1)],
        weights.at[1, core, pl.ds(0, ny - 1), x], weights.at[0, core, pl.ds(0, ny - 1)],
        weights.at[1, core, :, pl.ds(0, nx - 1)], weights.at[0],
        other_a.at[pl.ds(0, nx // 2)], other_a.at[pl.ds(0, nx // 2)],
        other_b.at[pl.ds(0, ny // 2)], other_b.at[pl.ds(0, ny // 2)],
        part_a.at[pl.ds(0, ny - 1)], part_b.at[pl.ds(0, nx - 1)],
        col_a.at[pl.ds(0, nx - 1)], col_b.at[pl.ds(0, ny - 1)], cell.at[pl.ds(0, nz - 1)],
        final.at[pl.ds(0, nd - 1)],
    )
    for phase, ref in enumerate(sent):
        drain(ref, sem_out.at[phase])


def store_out(hid_in, gs_in, gn_in, hid_ref, gs_ref, gn_ref, hid_buf, gs_buf, gn_buf, sems):
    bufs = (hid_buf, gs_buf, gn_buf)
    ins = [
        pltpu.make_async_copy(a, b, sems.at[i])
        for i, (a, b) in enumerate(zip((hid_in, gs_in, gn_in), bufs))
    ]
    outs = [
        pltpu.make_async_copy(a, b, sems.at[3 + i])
        for i, (a, b) in enumerate(zip(bufs, (hid_ref, gs_ref, gn_ref)))
    ]
    for copy in ins:
        copy.start()
    for i in range(3):
        ins[i].wait()
        outs[i].start()
    for copy in outs:
        copy.wait()


def on_device(features, w1, w2, cotangent, send_rows, send_count, tile_source, tile_kind, patterns):
    nx, nz = FEAT_GRID
    ny, nc = DOM_GRID
    nf, nd, hz = nx * nz, ny * nc, nz // 2
    width = features.shape[1]
    hidden = w1.shape[1]
    slot_tiles = send_rows.shape[2] // 128
    assert features.shape[0] == nf * 128 and hidden == ny * 128 and nc == 2
    band = hz * width
    vmem = pl.BlockSpec(memory_space=pltpu.VMEM)
    hbm = pl.BlockSpec(memory_space=pltpu.HBM)
    source, kind = tile_source[0].T, tile_kind[0].T
    shapes = (
        jax.ShapeDtypeStruct((128, hidden), BF),
        jax.ShapeDtypeStruct((width, hidden), F32),
        jax.ShapeDtypeStruct((width, hidden), F32),
    )
    results = pl.pallas_call(
        layer,
        out_shape=shapes,
        in_specs=[hbm] * 9,
        out_specs=(vmem,) * 3,
        scratch_shapes=[
            pltpu.VMEM((width, nf * 128), BF),
            pltpu.VMEM(send_rows.shape[1:], jnp.int32),
            pltpu.VMEM(patterns.shape, BF),
            pltpu.VMEM((128, hidden), BF),
            pltpu.SMEM(send_count.shape, jnp.int32),
            pltpu.SMEM(source.shape, jnp.int32),
            pltpu.SMEM(kind.shape, jnp.int32),
            pltpu.VMEM((nf + nd * slot_tiles, width, 128), BF),
            pltpu.VMEM((nd, slot_tiles, width, 128), BF),
            pltpu.VMEM((nf, width, 128), BF),
            pltpu.VMEM((2, nf, width, 128), BF),
            pltpu.VMEM((2, nc, ny, nx, hz, width, 128), BF),
            pltpu.VMEM((128, hidden), F32),
            pltpu.VMEM((128, hidden), BF),
            pltpu.VMEM((nx, ny, band, 128), BF),
            pltpu.VMEM((nx, ny, band, 128), BF),
            pltpu.VMEM((ny, nx, band, 128), BF),
            pltpu.VMEM((ny, nx, band, 128), BF),
            pltpu.VMEM((ny, nx, band, 128), BF),
            pltpu.VMEM((ny, nx, band, 128), BF),
            pltpu.VMEM((nx, ny, band, 128), BF),
            pltpu.VMEM((nx, ny, band, 128), BF),
            pltpu.VMEM((nx, band, 128), F32),
            pltpu.VMEM((ny, band, 128), F32),
            pltpu.VMEM((nx, band, 128), BF),
            pltpu.VMEM((nx, band, 128), BF),
            pltpu.VMEM((ny, band, 128), BF),
            pltpu.VMEM((ny, band, 128), BF),
            pltpu.VMEM((2, band, 128), F32),
            pltpu.VMEM((nz, width, 128), BF),
            pltpu.VMEM((nz, width, 128), BF),
            pltpu.VMEM((nd, width, 128), F32),
            pltpu.SemaphoreType.DMA((19,)),
            pltpu.SemaphoreType.DMA((19,)),
            pltpu.SemaphoreType.DMA((8,)),
            pltpu.SemaphoreType.REGULAR((3,)),
        ],
        compiler_params=pltpu.CompilerParams(
            collective_id=0, has_side_effects=True, vmem_limit_bytes=67_000_000
        ),
    )(
        features.T, w1, w2, cotangent, send_rows, patterns, send_count, source, kind,
    )
    return pl.pallas_call(
        store_out,
        out_shape=shapes,
        in_specs=[hbm] * 3,
        out_specs=(hbm,) * 3,
        scratch_shapes=[pltpu.VMEM(a.shape, a.dtype) for a in shapes]
        + [pltpu.SemaphoreType.DMA((6,))],
        compiler_params=pltpu.CompilerParams(vmem_limit_bytes=67_000_000),
    )(*results)


def solution(mesh):
    placed = (
        P("dom", "feat"),
        P("feat", None),
        P("feat", None),
        P(("dom", "feat"), None),
        P(),
        P(),
        P("dom", None, None),
        P("dom", None, None),
        P(),
    )
    return jax.shard_map(
        on_device,
        mesh=mesh,
        in_specs=placed,
        out_specs=(P(("dom", "feat"), None), P("feat", None), P("feat", None)),
        check_vma=False,
    )
```

```python
import jax
import jax.numpy as jnp
from jax import lax
from jax.experimental import pallas as pl
from jax.experimental.pallas import tpu as pltpu
from jax.sharding import PartitionSpec as P

FEAT_GRID = (4, 16)
DOM_GRID = (4, 2)
inv_root_two = 0.7071067811865476
inv_root_two_pi = 0.3989422804014327
BF = jnp.bfloat16
F32 = jnp.float32
MESH = pl.DeviceIdType.MESH


def gelu_pair(linear):
    normal_cdf = 0.5 * (1.0 + lax.erf(linear * inv_root_two))
    density = jnp.exp(-0.5 * linear * linear) * inv_root_two_pi
    return linear * normal_cdf, normal_cdf + linear * density


def drain(ref, sem):
    pltpu.make_async_copy(ref, ref, sem).wait()


def layer(
    x_hbm, w1_hbm, w2_hbm, cot_hbm, rows_hbm, pat_hbm, count_hbm, source_hbm, kind_hbm,
    hid_ref, gs_ref, gn_ref,
    x_own, wanted_ref, pats, cot, count_ref, source_ref, kind_ref,
    ext, halo_out, mean, by_z, xm, weights, partial, grad, other_a, other_a_in, other_b, other_b_in,
    part_a, part_a_in, part_b, part_b_in, kept_a, kept_b,
    col_a, col_a_in, col_b, col_b_in, fin, cell, cell_in, final,
    sem_out, sem_in, load_sem, round_sem,
):
    nx, nz = FEAT_GRID
    ny, nc = DOM_GRID
    nf, nd, hz = nx * nz, ny * nc, nz // 2
    feat = lax.axis_index("feat")
    dom = lax.axis_index("dom")
    x, z = feat // nz, feat % nz
    y, core = dom // nc, dom % nc
    half, zz = z // hz, z % hz
    width = x_own.shape[0]
    depth = nx * hz * width
    band = hz * width
    tiles = nf
    slot_tiles = halo_out.shape[1]
    slots = wanted_ref.shape[1]
    steps = source_ref.shape[0]

    def send(src, dst, phase, where):
        pltpu.make_async_remote_copy(
            src_ref=src, dst_ref=dst, send_sem=sem_out.at[phase], recv_sem=sem_in.at[phase],
            device_id=where, device_id_type=MESH,
        ).start()

    def feat_at(fx, fz):
        return {"feat": fx * nz + fz, "dom": dom}

    def dom_at(dy, dc):
        return {"feat": feat, "dom": dy * nc + dc}

    block = pl.ds(pl.multiple_of(y * 128, 128), 128)
    my_unit = weights.at[half, core, y, x, zz]
    loads = [
        pltpu.make_async_copy(src, dst, load_sem.at[i])
        for i, (src, dst) in enumerate((
            (x_hbm, x_own), (rows_hbm.at[dom], wanted_ref), (count_hbm, count_ref),
            (pat_hbm, pats), (source_hbm, source_ref), (kind_hbm, kind_ref), (cot_hbm, cot),
        ))
    ]
    barrier = pltpu.get_barrier_semaphore()

    def along(*distances):
        return sorted(({d % nz for d in distances} | {-d % nz for d in distances}) - {0})

    near = along(1, 2)
    for i in near:
        pl.semaphore_signal(barrier, inc=1, device_id=feat_at(x, (z + i) % nz), device_id_type=MESH)
    for i in range(1, nx):
        pl.semaphore_signal(barrier, inc=1, device_id=feat_at((x + i) % nx, z), device_id_type=MESH)
    for i in range(1, nd):
        pl.semaphore_signal(
            barrier, inc=1, device_id={"feat": feat, "dom": (dom + i) % nd}, device_id_type=MESH
        )

    def round_out(r, offsets):
        for i in offsets:
            pl.semaphore_signal(
                round_sem.at[r], inc=1, device_id=feat_at(x, (z + i) % nz), device_id_type=MESH
            )

    for load in loads:
        load.start()

    @pl.when(core == 0)
    def _():
        pltpu.make_async_copy(w1_hbm.at[:, block], my_unit, load_sem.at[7]).start()

    @pl.when(core == 1)
    def _():
        pltpu.make_async_copy(w2_hbm.at[:, block], my_unit, load_sem.at[7]).start()

    for load in loads[:3]:
        load.wait()

    def take(t, _):
        ext[t] = x_own[:, pl.ds(pl.multiple_of(t * 128, 128), 128)]
        return 0

    lax.fori_loop(0, tiles, take, 0)

    group = min(tiles, 16)
    lane_ids = lax.broadcasted_iota(jnp.int32, (128, slots), 0)
    slot_ids = lax.broadcasted_iota(jnp.int32, (1, slots), 1)

    halo_at = tiles + dom * slot_tiles

    def pick(i, _):
        dest = (dom + i) % nd
        wanted = wanted_ref[pl.ds(dest, 1), :]
        low, high = wanted & 127, wanted >> 7
        choose = jnp.where(lane_ids == low, 1.0, 0.0).astype(BF)
        found = jnp.zeros((width, slots), F32)
        for g in range(0, tiles, group):
            rows = ext[g : g + group].reshape(group * width, 128)
            spread = jnp.dot(rows, choose, preferred_element_type=F32)
            for h in range(group):
                found = jnp.where(
                    high == g + h, spread[h * width : (h + 1) * width], found
                )
        live = slot_ids < count_ref[dom, dest]
        found = jnp.where(live, found, 0.0).astype(BF)
        for j in range(slot_tiles):
            halo_out[dest, j] = found[:, j * 128 : (j + 1) * 128]

        @pl.when(dest != dom)
        def _():
            send(
                halo_out.at[dest], ext.at[pl.ds(halo_at, slot_tiles)], 0,
                {"feat": feat, "dom": dest},
            )

        return 0

    def x_send(m, tiles_at, phase, column):
        send(
            tiles_at.at[pl.ds(column * nz, nz)], by_z.at[m, :, x], phase, feat_at(column, z)
        )

    def z_sends(m, tiles_at, in_phase, out_phase):
        def keep(t, _):
            by_z[m, t, x] = tiles_at[x * nz + t]
            return 0

        def z_send(i, _):
            peer = (z + i) % nz
            send(by_z.at[m, peer], xm.at[m, half, zz], out_phase, feat_at(x, peer))
            return 0

        lax.fori_loop(0, nz, keep, 0)
        drain(tiles_at.at[pl.ds(0, (nx - 1) * nz)], sem_in.at[in_phase])
        lax.fori_loop(1, nz, z_send, 0)
        xm[m, half, zz] = by_z[m, z]

    assert nz <= 17
    pl.semaphore_wait(barrier, len(near) + nx - 1 + nd - 1)
    round_out(0, near)
    for i in range(1, nx):
        x_send(0, ext, 2, (x + i) % nx)
    lax.fori_loop(0, nd // 2, pick, 0)
    pltpu.make_async_copy(my_unit, my_unit, load_sem.at[7]).wait()
    pl.semaphore_wait(round_sem.at[0], len(near))
    middle = along(4)
    round_out(1, middle)
    lax.fori_loop(nd // 2, nd, pick, 0)
    for load in loads[3:]:
        load.wait()
    if middle:
        pl.semaphore_wait(round_sem.at[1], len(middle))

    def weights_z(i, _):
        send(my_unit, my_unit, 1, feat_at(x, (z + i) % nz))
        return 0

    lax.fori_loop(1, nz, weights_z, 0)
    z_sends(0, ext, 2, 19)
    for j in range(slot_tiles):
        ext[halo_at + j] = halo_out[dom, j]

    ones = jnp.ones((width, 256), BF)

    def mean_of(t):
        total = jnp.zeros((2 * width, 128), F32)
        for k in range(0, steps, 2):
            left = jnp.concatenate([ext[source_ref[k, t]], ext[source_ref[k + 1, t]]], axis=1)
            right = jnp.concatenate([pats[kind_ref[k, t]], pats[kind_ref[k + 1, t]]], axis=1)
            total = total + lax.dot_general(
                jnp.concatenate([left, ones], axis=0), right, (((1,), (1,)), ((), ())),
                preferred_element_type=F32,
            )
        return (total[:width] / total[width : width + 1]).astype(BF)

    drain(ext.at[pl.ds(tiles, (nd - 1) * slot_tiles)], sem_in.at[0])

    def column_out(g, _):
        column = (x + 1 + g) % nx

        def mean_pair(i, _):
            t = column * nz + 2 * i
            first, second = mean_of(t), mean_of(t + 1)
            mean[t] = first
            mean[t + 1] = second
            return 0

        lax.fori_loop(0, nz // 2, mean_pair, 0)

        @pl.when(column != x)
        def _():
            x_send(1, mean, 3, column)

        return 0

    lax.fori_loop(0, nx, column_out, 0)
    z_sends(1, mean, 3, 20)

    drain(ext.at[pl.ds(0, nz - 1)], sem_in.at[1])
    first_a, first_b = weights.at[0, core, y, x], weights.at[1, core, y, x]
    for i in range(1, nx):
        send(first_a, first_a, 4, feat_at((x + i) % nx, z))
    for i in range(1, ny):
        send(first_b, first_b, 5, dom_at((y + i) % ny, core))
    drain(weights.at[0, core, y, pl.ds(0, nx - 1)], sem_in.at[4])
    then_a = weights.at[0, core, y]
    for i in range(1, ny):
        send(then_a, then_a, 6, dom_at((y + i) % ny, core))
    drain(weights.at[1, core, pl.ds(0, ny - 1), x], sem_in.at[5])
    then_b = weights.at[1, core, :, x]
    for i in range(1, nx):
        send(then_b, then_b, 7, feat_at((x + i) % nx, z))
    drain(weights.at[0, core, pl.ds(0, ny - 1)], sem_in.at[6])
    drain(weights.at[1, core, :, pl.ds(0, nx - 1)], sem_in.at[7])
    for h in range(2):
        send(weights.at[h, core], weights.at[h, core], 8, dom_at(y, 1 - core))
    drain(by_z.at[0, pl.ds(0, nz - 1)], sem_in.at[19])

    def times_weights(m, own, b):
        total = jnp.zeros((128, 128), F32)
        for h in range(2):
            total = total + lax.dot_general(
                own[h], weights[h, m, b].reshape(depth, 128), (((0,), (0,)), ((), ())),
                preferred_element_type=F32,
            )
        return total

    def rows_of(m, h, b):
        return xm[m, h, :, b].reshape(band, 128)

    def halves(m):
        return [
            jnp.concatenate([rows_of(m, h, b) for b in range(nx)], axis=0) for h in range(2)
        ]

    drain(weights.at[0], sem_in.at[8])
    own = halves(0)
    for b in range(ny):
        partial[:, b * 128 : (b + 1) * 128] = times_weights(0, own, b)
    drain(by_z.at[1, pl.ds(0, nz - 1)], sem_in.at[20])
    own = halves(1)
    for b in range(ny):
        span = slice(b * 128, (b + 1) * 128)
        value, slope = gelu_pair(partial[:, span] + times_weights(1, own, b))
        hid_ref[:, span] = value.astype(BF)
        grad[:, span] = (cot[:, span].astype(F32) * slope).astype(BF)

    def product_a(m, b):
        return jnp.dot(rows_of(m, 0, b), grad[...], preferred_element_type=F32)

    def product_b(m, b, p):
        columns = grad[:, p * cb * 128 : (p + 1) * cb * 128]
        return jnp.dot(rows_of(m, 1, b), columns, preferred_element_type=F32)

    ca, cb = nx // 2, ny // 2
    for p in range(2):

        def core_a(b, _):
            result = product_a(1 - core, b).astype(BF)
            for c in range(ny):
                other_a[b, c] = result[:, c * 128 : (c + 1) * 128]
            return 0

        def core_b(b, _, p=p):
            result = product_b(1 - core, b, p).astype(BF)
            for c in range(cb):
                other_b[p * cb + c, b] = result[:, c * 128 : (c + 1) * 128]
            return 0

        lax.fori_loop(p * ca, (p + 1) * ca, core_a, 0)
        piece = pl.ds(p * ca, ca)
        send(other_a.at[piece], other_a_in.at[piece], 9 + p, dom_at(y, 1 - core))
        lax.fori_loop(0, nx, core_b, 0)
        piece = pl.ds(p * cb, cb)
        send(other_b.at[piece], other_b_in.at[piece], 11 + p, dom_at(y, 1 - core))

    for p in range(2):

        def y_first(b, _):
            result = product_a(core, b)
            for c in range(ny):
                summed = result[:, c * 128 : (c + 1) * 128] + other_a_in[b, c].astype(F32)
                part_a[c, b] = summed.astype(BF)

                @pl.when(c == y)
                def _():
                    kept_a[b] = summed

            return 0

        def x_first(b, _, p=p):
            result = product_b(core, b, p)
            for c in range(cb):
                column = p * cb + c
                summed = result[:, c * 128 : (c + 1) * 128] + other_b_in[column, b].astype(F32)
                part_b[b, column] = summed.astype(BF)

                @pl.when(b == x)
                def _():
                    kept_b[column] = summed

            return 0

        piece = pl.ds(p * ca, ca)
        drain(other_a_in.at[piece], sem_in.at[9 + p])
        lax.fori_loop(p * ca, (p + 1) * ca, y_first, 0)
        for i in range(1, ny):
            c = (y + i) % ny
            send(part_a.at[c, piece], part_a_in.at[y, piece], 13, dom_at(c, core))
        piece = pl.ds(p * cb, cb)
        drain(other_b_in.at[piece], sem_in.at[11 + p])
        lax.fori_loop(0, nx, x_first, 0)
        for i in range(1, nx):
            b = (x + i) % nx
            send(part_b.at[b, piece], part_b_in.at[x, piece], 14, feat_at(b, z))

    def y_sum(b):
        total = kept_a[b]
        for j in range(1, ny):
            total = total + part_a_in[(y + j) % ny, b].astype(F32)
        return total

    def x_sum(c):
        total = kept_b[c]
        for j in range(1, nx):
            total = total + part_b_in[(x + j) % nx, c].astype(F32)
        return total

    drain(part_a_in.at[pl.ds(0, ny - 1)], sem_in.at[13])

    def x_then(i, _):
        b = (x + i) % nx
        col_a[b] = y_sum(b).astype(BF)
        send(col_a.at[b], col_a_in.at[x], 15, feat_at(b, z))
        return 0

    lax.fori_loop(1, nx, x_then, 0)
    fin[0] = y_sum(x)

    drain(part_b_in.at[pl.ds(0, nx - 1)], sem_in.at[14])

    def y_then(i, _):
        c = (y + i) % ny
        col_b[c] = x_sum(c).astype(BF)
        send(col_b.at[c], col_b_in.at[y], 16, dom_at(c, core))
        return 0

    lax.fori_loop(1, ny, y_then, 0)
    fin[1] = x_sum(y)

    def z_out(i, _):
        peer = i

        @pl.when(peer != z)
        def _():
            send(cell.at[peer], cell_in.at[z], 17, feat_at(x, peer))

        return 0

    drain(col_a_in.at[pl.ds(0, nx - 1)], sem_in.at[15])
    total = fin[0]
    for j in range(1, nx):
        total = total + col_a_in[(x + j) % nx].astype(F32)
    fin[0] = total
    cell[0:hz] = total.astype(BF).reshape(hz, width, 128)
    lax.fori_loop(0, hz, z_out, 0)
    drain(col_b_in.at[pl.ds(0, ny - 1)], sem_in.at[16])
    total = fin[1]
    for j in range(1, ny):
        total = total + col_b_in[(y + j) % ny].astype(F32)
    fin[1] = total
    cell[hz:nz] = total.astype(BF).reshape(hz, width, 128)
    lax.fori_loop(hz, nz, z_out, 0)
    drain(cell_in.at[pl.ds(0, nz - 1)], sem_in.at[17])
    total = fin[half, pl.ds(pl.multiple_of(zz * width, width), width)]
    for j in range(1, nz):
        total = total + cell_in[(z + j) % nz].astype(F32)

    final[dom] = total

    def dom_out(i, _):
        send(final.at[dom], final.at[dom], 18, {"feat": feat, "dom": (dom + i) % nd})
        return 0

    lax.fori_loop(1, nd, dom_out, 0)
    drain(final.at[pl.ds(0, nd - 1)], sem_in.at[18])
    for b in range(ny):
        span = slice(b * 128, (b + 1) * 128)
        gs_ref[:, span] = final[b * nc]
        gn_ref[:, span] = final[b * nc + 1]

    sent = (
        halo_out.at[pl.ds(0, nd - 1)], ext.at[pl.ds(0, nz - 1)],
        ext.at[pl.ds(0, (nx - 1) * nz)], mean.at[pl.ds(0, (nx - 1) * nz)], weights.at[0, core, y, pl.ds(0, nx - 1)],
        weights.at[1, core, pl.ds(0, ny - 1), x], weights.at[0, core, pl.ds(0, ny - 1)],
        weights.at[1, core, :, pl.ds(0, nx - 1)], weights.at[0],
        other_a.at[pl.ds(0, nx // 2)], other_a.at[pl.ds(0, nx // 2)],
        other_b.at[pl.ds(0, ny // 2)], other_b.at[pl.ds(0, ny // 2)],
        part_a.at[pl.ds(0, ny - 1)], part_b.at[pl.ds(0, nx - 1)],
        col_a.at[pl.ds(0, nx - 1)], col_b.at[pl.ds(0, ny - 1)], cell.at[pl.ds(0, nz - 1)],
        final.at[pl.ds(0, nd - 1)], by_z.at[0, pl.ds(0, nz - 1)], by_z.at[1, pl.ds(0, nz - 1)],
    )
    for phase, ref in enumerate(sent):
        drain(ref, sem_out.at[phase])


def store_out(hid_in, gs_in, gn_in, hid_ref, gs_ref, gn_ref, hid_buf, gs_buf, gn_buf, sems):
    bufs = (hid_buf, gs_buf, gn_buf)
    ins = [
        pltpu.make_async_copy(a, b, sems.at[i])
        for i, (a, b) in enumerate(zip((hid_in, gs_in, gn_in), bufs))
    ]
    outs = [
        pltpu.make_async_copy(a, b, sems.at[3 + i])
        for i, (a, b) in enumerate(zip(bufs, (hid_ref, gs_ref, gn_ref)))
    ]
    for copy in ins:
        copy.start()
    for i in range(3):
        ins[i].wait()
        outs[i].start()
    for copy in outs:
        copy.wait()


def on_device(features, w1, w2, cotangent, send_rows, send_count, tile_source, tile_kind, patterns):
    nx, nz = FEAT_GRID
    ny, nc = DOM_GRID
    nf, nd, hz = nx * nz, ny * nc, nz // 2
    width = features.shape[1]
    hidden = w1.shape[1]
    slot_tiles = send_rows.shape[2] // 128
    assert features.shape[0] == nf * 128 and hidden == ny * 128 and nc == 2
    band = hz * width
    vmem = pl.BlockSpec(memory_space=pltpu.VMEM)
    hbm = pl.BlockSpec(memory_space=pltpu.HBM)
    source, kind = tile_source[0].T, tile_kind[0].T
    shapes = (
        jax.ShapeDtypeStruct((128, hidden), BF),
        jax.ShapeDtypeStruct((width, hidden), F32),
        jax.ShapeDtypeStruct((width, hidden), F32),
    )
    results = pl.pallas_call(
        layer,
        out_shape=shapes,
        in_specs=[hbm] * 9,
        out_specs=(vmem,) * 3,
        scratch_shapes=[
            pltpu.VMEM((width, nf * 128), BF),
            pltpu.VMEM(send_rows.shape[1:], jnp.int32),
            pltpu.VMEM(patterns.shape, BF),
            pltpu.VMEM((128, hidden), BF),
            pltpu.SMEM(send_count.shape, jnp.int32),
            pltpu.SMEM(source.shape, jnp.int32),
            pltpu.SMEM(kind.shape, jnp.int32),
            pltpu.VMEM((nf + nd * slot_tiles, width, 128), BF),
            pltpu.VMEM((nd, slot_tiles, width, 128), BF),
            pltpu.VMEM((nf, width, 128), BF),
            pltpu.VMEM((2, nz, nx, width, 128), BF),
            pltpu.VMEM((2, 2, hz, nx, width, 128), BF),
            pltpu.VMEM((2, nc, ny, nx, hz, width, 128), BF),
            pltpu.VMEM((128, hidden), F32),
            pltpu.VMEM((128, hidden), BF),
            pltpu.VMEM((nx, ny, band, 128), BF),
            pltpu.VMEM((nx, ny, band, 128), BF),
            pltpu.VMEM((ny, nx, band, 128), BF),
            pltpu.VMEM((ny, nx, band, 128), BF),
            pltpu.VMEM((ny, nx, band, 128), BF),
            pltpu.VMEM((ny, nx, band, 128), BF),
            pltpu.VMEM((nx, ny, band, 128), BF),
            pltpu.VMEM((nx, ny, band, 128), BF),
            pltpu.VMEM((nx, band, 128), F32),
            pltpu.VMEM((ny, band, 128), F32),
            pltpu.VMEM((nx, band, 128), BF),
            pltpu.VMEM((nx, band, 128), BF),
            pltpu.VMEM((ny, band, 128), BF),
            pltpu.VMEM((ny, band, 128), BF),
            pltpu.VMEM((2, band, 128), F32),
            pltpu.VMEM((nz, width, 128), BF),
            pltpu.VMEM((nz, width, 128), BF),
            pltpu.VMEM((nd, width, 128), F32),
            pltpu.SemaphoreType.DMA((21,)),
            pltpu.SemaphoreType.DMA((21,)),
            pltpu.SemaphoreType.DMA((8,)),
            pltpu.SemaphoreType.REGULAR((2,)),
        ],
        compiler_params=pltpu.CompilerParams(
            collective_id=0, has_side_effects=True, vmem_limit_bytes=67_000_000
        ),
    )(
        features.T, w1, w2, cotangent, send_rows, patterns, send_count, source, kind,
    )
    return pl.pallas_call(
        store_out,
        out_shape=shapes,
        in_specs=[hbm] * 3,
        out_specs=(hbm,) * 3,
        scratch_shapes=[pltpu.VMEM(a.shape, a.dtype) for a in shapes]
        + [pltpu.SemaphoreType.DMA((6,))],
        compiler_params=pltpu.CompilerParams(vmem_limit_bytes=67_000_000),
    )(*results)


def solution(mesh):
    placed = (
        P("dom", "feat"),
        P("feat", None),
        P("feat", None),
        P(("dom", "feat"), None),
        P(),
        P(),
        P("dom", None, None),
        P("dom", None, None),
        P(),
    )
    return jax.shard_map(
        on_device,
        mesh=mesh,
        in_specs=placed,
        out_specs=(P(("dom", "feat"), None), P("feat", None), P("feat", None)),
        check_vma=False,
    )
```

```python
import jax
import jax.numpy as jnp
from jax import lax
from jax.experimental import pallas as pl
from jax.experimental.pallas import tpu as pltpu
from jax.sharding import PartitionSpec as P

FEAT_GRID = (4, 16)
DOM_GRID = (4, 2)
inv_root_two = 0.7071067811865476
inv_root_two_pi = 0.3989422804014327
BF = jnp.bfloat16
F32 = jnp.float32
MESH = pl.DeviceIdType.MESH


def gelu_pair(linear):
    normal_cdf = 0.5 * (1.0 + lax.erf(linear * inv_root_two))
    density = jnp.exp(-0.5 * linear * linear) * inv_root_two_pi
    return linear * normal_cdf, normal_cdf + linear * density


def drain(ref, sem):
    pltpu.make_async_copy(ref, ref, sem).wait()


def layer(
    x_hbm, w1_hbm, w2_hbm, cot_hbm, rows_hbm, pat_hbm, count_hbm, source_hbm, kind_hbm,
    hid_ref, gs_ref, gn_ref,
    x_own, wanted_ref, pats, cot, count_ref, source_ref, kind_ref,
    ext, halo_out, mean, by_z, xm, weights, partial, grad, other_a, other_a_in, other_b, other_b_in,
    part_a, part_a_in, part_b, part_b_in, kept_a, kept_b,
    col_a, col_a_in, col_b, col_b_in, fin, cell, cell_in, final,
    sem_out, sem_in, load_sem, round_sem,
):
    nx, nz = FEAT_GRID
    ny, nc = DOM_GRID
    nf, nd, hz = nx * nz, ny * nc, nz // 2
    feat = lax.axis_index("feat")
    dom = lax.axis_index("dom")
    x, z = feat // nz, feat % nz
    y, core = dom // nc, dom % nc
    half, zz = z // hz, z % hz
    width = x_own.shape[0]
    depth = nx * hz * width
    band = hz * width
    tiles = nf
    slot_tiles = halo_out.shape[1]
    slots = wanted_ref.shape[1]
    steps = source_ref.shape[0]

    def send(src, dst, phase, where):
        pltpu.make_async_remote_copy(
            src_ref=src, dst_ref=dst, send_sem=sem_out.at[phase], recv_sem=sem_in.at[phase],
            device_id=where, device_id_type=MESH,
        ).start()

    def feat_at(fx, fz):
        return {"feat": fx * nz + fz, "dom": dom}

    def dom_at(dy, dc):
        return {"feat": feat, "dom": dy * nc + dc}

    block = pl.ds(pl.multiple_of(y * 128, 128), 128)
    my_unit = weights.at[half, core, y, x, zz]
    loads = [
        pltpu.make_async_copy(src, dst, load_sem.at[i])
        for i, (src, dst) in enumerate((
            (x_hbm, x_own), (rows_hbm.at[dom], wanted_ref), (count_hbm, count_ref),
            (pat_hbm, pats), (source_hbm, source_ref), (kind_hbm, kind_ref), (cot_hbm, cot),
        ))
    ]
    barrier = pltpu.get_barrier_semaphore()

    def along(*distances):
        return sorted(({d % nz for d in distances} | {-d % nz for d in distances}) - {0})

    near = along(1, 2)
    for i in near:
        pl.semaphore_signal(barrier, inc=1, device_id=feat_at(x, (z + i) % nz), device_id_type=MESH)
    for i in range(1, nx):
        pl.semaphore_signal(barrier, inc=1, device_id=feat_at((x + i) % nx, z), device_id_type=MESH)
    for i in range(1, nd):
        pl.semaphore_signal(
            barrier, inc=1, device_id={"feat": feat, "dom": (dom + i) % nd}, device_id_type=MESH
        )

    def round_out(r, offsets):
        for i in offsets:
            pl.semaphore_signal(
                round_sem.at[r], inc=1, device_id=feat_at(x, (z + i) % nz), device_id_type=MESH
            )

    for load in loads:
        load.start()

    @pl.when(core == 0)
    def _():
        pltpu.make_async_copy(w1_hbm.at[:, block], my_unit, load_sem.at[7]).start()

    @pl.when(core == 1)
    def _():
        pltpu.make_async_copy(w2_hbm.at[:, block], my_unit, load_sem.at[7]).start()

    for load in loads[:3]:
        load.wait()

    def take(t, _):
        ext[t] = x_own[:, pl.ds(pl.multiple_of(t * 128, 128), 128)]
        return 0

    lax.fori_loop(0, tiles, take, 0)

    group = min(tiles, 16)
    lane_ids = lax.broadcasted_iota(jnp.int32, (128, slots), 0)
    slot_ids = lax.broadcasted_iota(jnp.int32, (1, slots), 1)

    halo_at = tiles + dom * slot_tiles

    def pick(i, _):
        dest = (dom + i) % nd
        wanted = wanted_ref[pl.ds(dest, 1), :]
        low, high = wanted & 127, wanted >> 7
        choose = jnp.where(lane_ids == low, 1.0, 0.0).astype(BF)
        found = jnp.zeros((width, slots), F32)
        for g in range(0, tiles, group):
            rows = ext[g : g + group].reshape(group * width, 128)
            spread = jnp.dot(rows, choose, preferred_element_type=F32)
            for h in range(group):
                found = jnp.where(
                    high == g + h, spread[h * width : (h + 1) * width], found
                )
        live = slot_ids < count_ref[dom, dest]
        found = jnp.where(live, found, 0.0).astype(BF)
        for j in range(slot_tiles):
            halo_out[dest, j] = found[:, j * 128 : (j + 1) * 128]

        @pl.when(dest != dom)
        def _():
            send(
                halo_out.at[dest], ext.at[pl.ds(halo_at, slot_tiles)], 0,
                {"feat": feat, "dom": dest},
            )

        return 0

    outward = sorted(range(1, nz), key=lambda i: (-min(i, nz - i), i))

    def x_send(m, tiles_at, phase, column):
        send(
            tiles_at.at[pl.ds(column * nz, nz)], by_z.at[m, :, x], phase, feat_at(column, z)
        )

    def z_sends(m, tiles_at, in_phase, out_phase):
        def keep(t, _):
            by_z[m, t, x] = tiles_at[x * nz + t]
            return 0

        lax.fori_loop(0, nz, keep, 0)
        drain(tiles_at.at[pl.ds(0, (nx - 1) * nz)], sem_in.at[in_phase])
        for i in outward:
            peer = (z + i) % nz
            send(by_z.at[m, peer], xm.at[m, half, zz], out_phase, feat_at(x, peer))
        xm[m, half, zz] = by_z[m, z]

    assert nz <= 17
    pl.semaphore_wait(barrier, len(near) + nx - 1 + nd - 1)
    round_out(0, near)
    for i in range(1, nx):
        x_send(0, ext, 2, (x + i) % nx)
    lax.fori_loop(0, nd // 2, pick, 0)
    pltpu.make_async_copy(my_unit, my_unit, load_sem.at[7]).wait()
    pl.semaphore_wait(round_sem.at[0], len(near))
    middle = along(4)
    round_out(1, middle)
    lax.fori_loop(nd // 2, nd, pick, 0)
    for load in loads[3:]:
        load.wait()
    if middle:
        pl.semaphore_wait(round_sem.at[1], len(middle))

    for i in outward:
        send(my_unit, my_unit, 1, feat_at(x, (z + i) % nz))
    z_sends(0, ext, 2, 19)
    for j in range(slot_tiles):
        ext[halo_at + j] = halo_out[dom, j]

    ones = jnp.ones((width, 256), BF)

    def mean_of(t):
        total = jnp.zeros((2 * width, 128), F32)
        for k in range(0, steps, 2):
            left = jnp.concatenate([ext[source_ref[k, t]], ext[source_ref[k + 1, t]]], axis=1)
            right = jnp.concatenate([pats[kind_ref[k, t]], pats[kind_ref[k + 1, t]]], axis=1)
            total = total + lax.dot_general(
                jnp.concatenate([left, ones], axis=0), right, (((1,), (1,)), ((), ())),
                preferred_element_type=F32,
            )
        return (total[:width] / total[width : width + 1]).astype(BF)

    drain(ext.at[pl.ds(tiles, (nd - 1) * slot_tiles)], sem_in.at[0])

    def column_out(g, _):
        column = (x + 1 + g) % nx

        def mean_pair(i, _):
            t = column * nz + 2 * i
            first, second = mean_of(t), mean_of(t + 1)
            mean[t] = first
            mean[t + 1] = second
            return 0

        lax.fori_loop(0, nz // 2, mean_pair, 0)

        @pl.when(column != x)
        def _():
            x_send(1, mean, 3, column)

        return 0

    lax.fori_loop(0, nx, column_out, 0)
    z_sends(1, mean, 3, 20)

    drain(ext.at[pl.ds(0, nz - 1)], sem_in.at[1])
    first_a, first_b = weights.at[0, core, y, x], weights.at[1, core, y, x]
    for i in range(1, nx):
        send(first_a, first_a, 4, feat_at((x + i) % nx, z))
    for i in range(1, ny):
        send(first_b, first_b, 5, dom_at((y + i) % ny, core))
    drain(weights.at[0, core, y, pl.ds(0, nx - 1)], sem_in.at[4])
    then_a = weights.at[0, core, y]
    for i in range(1, ny):
        send(then_a, then_a, 6, dom_at((y + i) % ny, core))
    drain(weights.at[1, core, pl.ds(0, ny - 1), x], sem_in.at[5])
    then_b = weights.at[1, core, :, x]
    for i in range(1, nx):
        send(then_b, then_b, 7, feat_at((x + i) % nx, z))
    drain(weights.at[0, core, pl.ds(0, ny - 1)], sem_in.at[6])
    drain(weights.at[1, core, :, pl.ds(0, nx - 1)], sem_in.at[7])
    for h in range(2):
        send(weights.at[h, core], weights.at[h, core], 8, dom_at(y, 1 - core))
    drain(by_z.at[0, pl.ds(0, nz - 1)], sem_in.at[19])

    def times_weights(m, own, b):
        total = jnp.zeros((128, 128), F32)
        for h in range(2):
            total = total + lax.dot_general(
                own[h], weights[h, m, b].reshape(depth, 128), (((0,), (0,)), ((), ())),
                preferred_element_type=F32,
            )
        return total

    def rows_of(m, h, b):
        return xm[m, h, :, b].reshape(band, 128)

    def halves(m):
        return [
            jnp.concatenate([rows_of(m, h, b) for b in range(nx)], axis=0) for h in range(2)
        ]

    drain(weights.at[0], sem_in.at[8])
    own = halves(0)
    for b in range(ny):
        partial[:, b * 128 : (b + 1) * 128] = times_weights(0, own, b)
    drain(by_z.at[1, pl.ds(0, nz - 1)], sem_in.at[20])
    own = halves(1)
    for b in range(ny):
        span = slice(b * 128, (b + 1) * 128)
        value, slope = gelu_pair(partial[:, span] + times_weights(1, own, b))
        hid_ref[:, span] = value.astype(BF)
        grad[:, span] = (cot[:, span].astype(F32) * slope).astype(BF)

    def product_a(m, b):
        return jnp.dot(rows_of(m, 0, b), grad[...], preferred_element_type=F32)

    def product_b(m, b, p):
        columns = grad[:, p * cb * 128 : (p + 1) * cb * 128]
        return jnp.dot(rows_of(m, 1, b), columns, preferred_element_type=F32)

    ca, cb = nx // 2, ny // 2
    for p in range(2):

        def core_a(b, _):
            result = product_a(1 - core, b).astype(BF)
            for c in range(ny):
                other_a[b, c] = result[:, c * 128 : (c + 1) * 128]
            return 0

        def core_b(b, _, p=p):
            result = product_b(1 - core, b, p).astype(BF)
            for c in range(cb):
                other_b[p * cb + c, b] = result[:, c * 128 : (c + 1) * 128]
            return 0

        lax.fori_loop(p * ca, (p + 1) * ca, core_a, 0)
        piece = pl.ds(p * ca, ca)
        send(other_a.at[piece], other_a_in.at[piece], 9 + p, dom_at(y, 1 - core))
        lax.fori_loop(0, nx, core_b, 0)
        piece = pl.ds(p * cb, cb)
        send(other_b.at[piece], other_b_in.at[piece], 11 + p, dom_at(y, 1 - core))

    for p in range(2):

        def y_first(b, _):
            result = product_a(core, b)
            for c in range(ny):
                summed = result[:, c * 128 : (c + 1) * 128] + other_a_in[b, c].astype(F32)
                part_a[c, b] = summed.astype(BF)

                @pl.when(c == y)
                def _():
                    kept_a[b] = summed

            return 0

        def x_first(b, _, p=p):
            result = product_b(core, b, p)
            for c in range(cb):
                column = p * cb + c
                summed = result[:, c * 128 : (c + 1) * 128] + other_b_in[column, b].astype(F32)
                part_b[b, column] = summed.astype(BF)

                @pl.when(b == x)
                def _():
                    kept_b[column] = summed

            return 0

        piece = pl.ds(p * ca, ca)
        drain(other_a_in.at[piece], sem_in.at[9 + p])
        lax.fori_loop(p * ca, (p + 1) * ca, y_first, 0)
        for i in range(1, ny):
            c = (y + i) % ny
            send(part_a.at[c, piece], part_a_in.at[y, piece], 13, dom_at(c, core))
        piece = pl.ds(p * cb, cb)
        drain(other_b_in.at[piece], sem_in.at[11 + p])
        lax.fori_loop(0, nx, x_first, 0)
        for i in range(1, nx):
            b = (x + i) % nx
            send(part_b.at[b, piece], part_b_in.at[x, piece], 14, feat_at(b, z))

    def y_sum(b):
        total = kept_a[b]
        for j in range(1, ny):
            total = total + part_a_in[(y + j) % ny, b].astype(F32)
        return total

    def x_sum(c):
        total = kept_b[c]
        for j in range(1, nx):
            total = total + part_b_in[(x + j) % nx, c].astype(F32)
        return total

    drain(part_a_in.at[pl.ds(0, ny - 1)], sem_in.at[13])

    def x_then(i, _):
        b = (x + i) % nx
        col_a[b] = y_sum(b).astype(BF)
        send(col_a.at[b], col_a_in.at[x], 15, feat_at(b, z))
        return 0

    lax.fori_loop(1, nx, x_then, 0)
    fin[0] = y_sum(x)

    drain(part_b_in.at[pl.ds(0, nx - 1)], sem_in.at[14])

    def y_then(i, _):
        c = (y + i) % ny
        col_b[c] = x_sum(c).astype(BF)
        send(col_b.at[c], col_b_in.at[y], 16, dom_at(c, core))
        return 0

    lax.fori_loop(1, ny, y_then, 0)
    fin[1] = x_sum(y)

    def z_out(h):
        for i in outward:
            peer = (z + i) % nz

            @pl.when(peer // hz == h)
            def _(peer=peer):
                send(cell.at[peer], cell_in.at[z], 17, feat_at(x, peer))

    drain(col_a_in.at[pl.ds(0, nx - 1)], sem_in.at[15])
    total = fin[0]
    for j in range(1, nx):
        total = total + col_a_in[(x + j) % nx].astype(F32)
    fin[0] = total
    cell[0:hz] = total.astype(BF).reshape(hz, width, 128)
    z_out(0)
    drain(col_b_in.at[pl.ds(0, ny - 1)], sem_in.at[16])
    total = fin[1]
    for j in range(1, ny):
        total = total + col_b_in[(y + j) % ny].astype(F32)
    fin[1] = total
    cell[hz:nz] = total.astype(BF).reshape(hz, width, 128)
    z_out(1)
    drain(cell_in.at[pl.ds(0, nz - 1)], sem_in.at[17])
    total = fin[half, pl.ds(pl.multiple_of(zz * width, width), width)]
    for j in range(1, nz):
        total = total + cell_in[(z + j) % nz].astype(F32)

    final[dom] = total

    def dom_out(i, _):
        send(final.at[dom], final.at[dom], 18, {"feat": feat, "dom": (dom + i) % nd})
        return 0

    lax.fori_loop(1, nd, dom_out, 0)
    drain(final.at[pl.ds(0, nd - 1)], sem_in.at[18])
    for b in range(ny):
        span = slice(b * 128, (b + 1) * 128)
        gs_ref[:, span] = final[b * nc]
        gn_ref[:, span] = final[b * nc + 1]

    sent = (
        halo_out.at[pl.ds(0, nd - 1)], ext.at[pl.ds(0, nz - 1)],
        ext.at[pl.ds(0, (nx - 1) * nz)], mean.at[pl.ds(0, (nx - 1) * nz)], weights.at[0, core, y, pl.ds(0, nx - 1)],
        weights.at[1, core, pl.ds(0, ny - 1), x], weights.at[0, core, pl.ds(0, ny - 1)],
        weights.at[1, core, :, pl.ds(0, nx - 1)], weights.at[0],
        other_a.at[pl.ds(0, nx // 2)], other_a.at[pl.ds(0, nx // 2)],
        other_b.at[pl.ds(0, ny // 2)], other_b.at[pl.ds(0, ny // 2)],
        part_a.at[pl.ds(0, ny - 1)], part_b.at[pl.ds(0, nx - 1)],
        col_a.at[pl.ds(0, nx - 1)], col_b.at[pl.ds(0, ny - 1)], cell.at[pl.ds(0, nz - 1)],
        final.at[pl.ds(0, nd - 1)], by_z.at[0, pl.ds(0, nz - 1)], by_z.at[1, pl.ds(0, nz - 1)],
    )
    for phase, ref in enumerate(sent):
        drain(ref, sem_out.at[phase])


def store_out(hid_in, gs_in, gn_in, hid_ref, gs_ref, gn_ref, hid_buf, gs_buf, gn_buf, sems):
    bufs = (hid_buf, gs_buf, gn_buf)
    ins = [
        pltpu.make_async_copy(a, b, sems.at[i])
        for i, (a, b) in enumerate(zip((hid_in, gs_in, gn_in), bufs))
    ]
    outs = [
        pltpu.make_async_copy(a, b, sems.at[3 + i])
        for i, (a, b) in enumerate(zip(bufs, (hid_ref, gs_ref, gn_ref)))
    ]
    for copy in ins:
        copy.start()
    for i in range(3):
        ins[i].wait()
        outs[i].start()
    for copy in outs:
        copy.wait()


def on_device(features, w1, w2, cotangent, send_rows, send_count, tile_source, tile_kind, patterns):
    nx, nz = FEAT_GRID
    ny, nc = DOM_GRID
    nf, nd, hz = nx * nz, ny * nc, nz // 2
    width = features.shape[1]
    hidden = w1.shape[1]
    slot_tiles = send_rows.shape[2] // 128
    assert features.shape[0] == nf * 128 and hidden == ny * 128 and nc == 2
    band = hz * width
    vmem = pl.BlockSpec(memory_space=pltpu.VMEM)
    hbm = pl.BlockSpec(memory_space=pltpu.HBM)
    source, kind = tile_source[0].T, tile_kind[0].T
    shapes = (
        jax.ShapeDtypeStruct((128, hidden), BF),
        jax.ShapeDtypeStruct((width, hidden), F32),
        jax.ShapeDtypeStruct((width, hidden), F32),
    )
    results = pl.pallas_call(
        layer,
        out_shape=shapes,
        in_specs=[hbm] * 9,
        out_specs=(vmem,) * 3,
        scratch_shapes=[
            pltpu.VMEM((width, nf * 128), BF),
            pltpu.VMEM(send_rows.shape[1:], jnp.int32),
            pltpu.VMEM(patterns.shape, BF),
            pltpu.VMEM((128, hidden), BF),
            pltpu.SMEM(send_count.shape, jnp.int32),
            pltpu.SMEM(source.shape, jnp.int32),
            pltpu.SMEM(kind.shape, jnp.int32),
            pltpu.VMEM((nf + nd * slot_tiles, width, 128), BF),
            pltpu.VMEM((nd, slot_tiles, width, 128), BF),
            pltpu.VMEM((nf, width, 128), BF),
            pltpu.VMEM((2, nz, nx, width, 128), BF),
            pltpu.VMEM((2, 2, hz, nx, width, 128), BF),
            pltpu.VMEM((2, nc, ny, nx, hz, width, 128), BF),
            pltpu.VMEM((128, hidden), F32),
            pltpu.VMEM((128, hidden), BF),
            pltpu.VMEM((nx, ny, band, 128), BF),
            pltpu.VMEM((nx, ny, band, 128), BF),
            pltpu.VMEM((ny, nx, band, 128), BF),
            pltpu.VMEM((ny, nx, band, 128), BF),
            pltpu.VMEM((ny, nx, band, 128), BF),
            pltpu.VMEM((ny, nx, band, 128), BF),
            pltpu.VMEM((nx, ny, band, 128), BF),
            pltpu.VMEM((nx, ny, band, 128), BF),
            pltpu.VMEM((nx, band, 128), F32),
            pltpu.VMEM((ny, band, 128), F32),
            pltpu.VMEM((nx, band, 128), BF),
            pltpu.VMEM((nx, band, 128), BF),
            pltpu.VMEM((ny, band, 128), BF),
            pltpu.VMEM((ny, band, 128), BF),
            pltpu.VMEM((2, band, 128), F32),
            pltpu.VMEM((nz, width, 128), BF),
            pltpu.VMEM((nz, width, 128), BF),
            pltpu.VMEM((nd, width, 128), F32),
            pltpu.SemaphoreType.DMA((21,)),
            pltpu.SemaphoreType.DMA((21,)),
            pltpu.SemaphoreType.DMA((8,)),
            pltpu.SemaphoreType.REGULAR((2,)),
        ],
        compiler_params=pltpu.CompilerParams(
            collective_id=0, has_side_effects=True, vmem_limit_bytes=67_000_000
        ),
    )(
        features.T, w1, w2, cotangent, send_rows, patterns, send_count, source, kind,
    )
    return pl.pallas_call(
        store_out,
        out_shape=shapes,
        in_specs=[hbm] * 3,
        out_specs=(hbm,) * 3,
        scratch_shapes=[pltpu.VMEM(a.shape, a.dtype) for a in shapes]
        + [pltpu.SemaphoreType.DMA((6,))],
        compiler_params=pltpu.CompilerParams(vmem_limit_bytes=67_000_000),
    )(*results)


def solution(mesh):
    placed = (
        P("dom", "feat"),
        P("feat", None),
        P("feat", None),
        P(("dom", "feat"), None),
        P(),
        P(),
        P("dom", None, None),
        P("dom", None, None),
        P(),
    )
    return jax.shard_map(
        on_device,
        mesh=mesh,
        in_specs=placed,
        out_specs=(P(("dom", "feat"), None), P("feat", None), P("feat", None)),
        check_vma=False,
    )
```

```python
import jax
import jax.numpy as jnp
from jax import lax
from jax.experimental import pallas as pl
from jax.experimental.pallas import tpu as pltpu
from jax.sharding import PartitionSpec as P

FEAT_GRID = (4, 16)
DOM_GRID = (4, 2)
inv_root_two = 0.7071067811865476
inv_root_two_pi = 0.3989422804014327
BF = jnp.bfloat16
F32 = jnp.float32
MESH = pl.DeviceIdType.MESH


def gelu_pair(linear):
    normal_cdf = 0.5 * (1.0 + lax.erf(linear * inv_root_two))
    density = jnp.exp(-0.5 * linear * linear) * inv_root_two_pi
    return linear * normal_cdf, normal_cdf + linear * density


def drain(ref, sem):
    pltpu.make_async_copy(ref, ref, sem).wait()


def layer(
    x_hbm, w1_hbm, w2_hbm, cot_hbm, rows_hbm, pat_hbm, count_hbm, source_hbm, kind_hbm,
    hid_ref, gs_ref, gn_ref,
    x_own, wanted_ref, pats, cot, count_ref, source_ref, kind_ref,
    ext, halo_out, mean, by_z, xm, weights, partial, grad, other_a, other_a_in, other_b, other_b_in,
    part_a, part_a_in, part_b, part_b_in, kept_a, kept_b,
    col_a, col_a_in, col_b, col_b_in, fin, cell, cell_in, final,
    sem_out, sem_in, load_sem, round_sem,
):
    nx, nz = FEAT_GRID
    ny, nc = DOM_GRID
    nf, nd, hz = nx * nz, ny * nc, nz // 2
    feat = lax.axis_index("feat")
    dom = lax.axis_index("dom")
    x, z = feat // nz, feat % nz
    y, core = dom // nc, dom % nc
    half, zz = z // hz, z % hz
    width = x_own.shape[0]
    depth = nx * hz * width
    band = hz * width
    tiles = nf
    slot_tiles = halo_out.shape[1]
    slots = wanted_ref.shape[1]
    steps = source_ref.shape[0]

    def send(src, dst, phase, where):
        pltpu.make_async_remote_copy(
            src_ref=src, dst_ref=dst, send_sem=sem_out.at[phase], recv_sem=sem_in.at[phase],
            device_id=where, device_id_type=MESH,
        ).start()

    def feat_at(fx, fz):
        return {"feat": fx * nz + fz, "dom": dom}

    def dom_at(dy, dc):
        return {"feat": feat, "dom": dy * nc + dc}

    block = pl.ds(pl.multiple_of(y * 128, 128), 128)
    my_unit = weights.at[half, core, y, x, zz]
    loads = [
        pltpu.make_async_copy(src, dst, load_sem.at[i])
        for i, (src, dst) in enumerate((
            (x_hbm, x_own), (rows_hbm.at[dom], wanted_ref), (count_hbm, count_ref),
            (pat_hbm, pats), (source_hbm, source_ref), (kind_hbm, kind_ref), (cot_hbm, cot),
        ))
    ]
    barrier = pltpu.get_barrier_semaphore()

    def along(*distances):
        return sorted(({d % nz for d in distances} | {-d % nz for d in distances}) - {0})

    near = along(1, 2)
    for i in near:
        pl.semaphore_signal(barrier, inc=1, device_id=feat_at(x, (z + i) % nz), device_id_type=MESH)
    for i in range(1, nx):
        pl.semaphore_signal(barrier, inc=1, device_id=feat_at((x + i) % nx, z), device_id_type=MESH)
    for i in range(1, nd):
        pl.semaphore_signal(
            barrier, inc=1, device_id={"feat": feat, "dom": (dom + i) % nd}, device_id_type=MESH
        )

    def round_out(r, offsets):
        for i in offsets:
            pl.semaphore_signal(
                round_sem.at[r], inc=1, device_id=feat_at(x, (z + i) % nz), device_id_type=MESH
            )

    for load in loads:
        load.start()

    @pl.when(core == 0)
    def _():
        pltpu.make_async_copy(w1_hbm.at[:, block], my_unit, load_sem.at[7]).start()

    @pl.when(core == 1)
    def _():
        pltpu.make_async_copy(w2_hbm.at[:, block], my_unit, load_sem.at[7]).start()

    for load in loads[:3]:
        load.wait()

    def take(t, _):
        ext[t] = x_own[:, pl.ds(pl.multiple_of(t * 128, 128), 128)]
        return 0

    lax.fori_loop(0, tiles, take, 0)

    group = min(tiles, 16)
    lane_ids = lax.broadcasted_iota(jnp.int32, (128, slots), 0)
    slot_ids = lax.broadcasted_iota(jnp.int32, (1, slots), 1)

    halo_at = tiles + dom * slot_tiles

    def pick(i, _):
        dest = (dom + i) % nd
        wanted = wanted_ref[pl.ds(dest, 1), :]
        low, high = wanted & 127, wanted >> 7
        choose = jnp.where(lane_ids == low, 1.0, 0.0).astype(BF)
        found = jnp.zeros((width, slots), F32)
        for g in range(0, tiles, group):
            rows = ext[g : g + group].reshape(group * width, 128)
            spread = jnp.dot(rows, choose, preferred_element_type=F32)
            for h in range(group):
                found = jnp.where(
                    high == g + h, spread[h * width : (h + 1) * width], found
                )
        live = slot_ids < count_ref[dom, dest]
        found = jnp.where(live, found, 0.0).astype(BF)
        for j in range(slot_tiles):
            halo_out[dest, j] = found[:, j * 128 : (j + 1) * 128]

        @pl.when(dest != dom)
        def _():
            send(
                halo_out.at[dest], ext.at[pl.ds(halo_at, slot_tiles)], 0,
                {"feat": feat, "dom": dest},
            )

        return 0

    def ring(n):
        return sorted(range(1, n), key=lambda i: (-min(i, n - i), i))

    outward = ring(nz)

    def x_send(m, tiles_at, phase, i):
        column = (x + i) % nx
        send(
            tiles_at.at[pl.ds(column * nz, nz)], by_z.at[m, :, nx - i], phase, feat_at(column, z)
        )

    def z_first(least, most):
        for i in outward:
            if least < min(i, nz - i) <= most:
                peer = (z + i) % nz
                send(my_unit, my_unit, 1, feat_at(x, peer))
                send(ext.at[x * nz + peer], xm.at[0, half, zz, 0], 21, feat_at(x, peer))

    assert nz <= 17
    pltpu.make_async_copy(my_unit, my_unit, load_sem.at[7]).wait()
    pl.semaphore_wait(barrier, len(near) + nx - 1 + nd - 1)
    round_out(0, near)
    for i in ring(nx):
        x_send(0, ext, 2, i)
    z_first(0, 2)
    lax.fori_loop(0, nd // 2, pick, 0)
    pl.semaphore_wait(round_sem.at[0], len(near))
    middle = along(4)
    round_out(1, middle)
    z_first(2, 4)
    lax.fori_loop(nd // 2, nd, pick, 0)
    for load in loads[3:]:
        load.wait()
    if middle:
        pl.semaphore_wait(round_sem.at[1], len(middle))
    z_first(4, nz)
    xm[0, half, zz, 0] = ext[feat]
    drain(ext.at[pl.ds(0, (nx - 1) * nz)], sem_in.at[2])
    others = pl.ds(1, nx - 1)
    for i in outward:
        peer = (z + i) % nz
        send(by_z.at[0, peer, others], xm.at[0, half, zz, others], 19, feat_at(x, peer))
    for j in range(1, nx):
        xm[0, half, zz, j] = by_z[0, z, j]
    for j in range(slot_tiles):
        ext[halo_at + j] = halo_out[dom, j]

    ones = jnp.ones((width, 256), BF)

    def mean_of(t):
        total = jnp.zeros((2 * width, 128), F32)
        for k in range(0, steps, 2):
            left = jnp.concatenate([ext[source_ref[k, t]], ext[source_ref[k + 1, t]]], axis=1)
            right = jnp.concatenate([pats[kind_ref[k, t]], pats[kind_ref[k + 1, t]]], axis=1)
            total = total + lax.dot_general(
                jnp.concatenate([left, ones], axis=0), right, (((1,), (1,)), ((), ())),
                preferred_element_type=F32,
            )
        return (total[:width] / total[width : width + 1]).astype(BF)

    drain(ext.at[pl.ds(tiles, (nd - 1) * slot_tiles)], sem_in.at[0])

    def column_means(column):
        def mean_pair(i, _):
            t = column * nz + 2 * i
            first, second = mean_of(t), mean_of(t + 1)
            mean[t] = first
            mean[t + 1] = second
            return 0

        lax.fori_loop(0, nz // 2, mean_pair, 0)

    def column_out(i, _):
        column_means((x + i) % nx)
        x_send(1, mean, 3, i)
        return 0

    lax.fori_loop(1, nx, column_out, 0)
    column_means(x)

    def keep(t, _):
        by_z[1, t, 0] = mean[x * nz + t]
        return 0

    lax.fori_loop(0, nz, keep, 0)
    drain(mean.at[pl.ds(0, (nx - 1) * nz)], sem_in.at[3])
    for i in outward:
        peer = (z + i) % nz
        send(by_z.at[1, peer], xm.at[1, half, zz], 20, feat_at(x, peer))
    xm[1, half, zz] = by_z[1, z]

    drain(ext.at[pl.ds(0, nz - 1)], sem_in.at[1])
    first_a, first_b = weights.at[0, core, y, x], weights.at[1, core, y, x]
    for i in ring(nx):
        send(first_a, first_a, 4, feat_at((x + i) % nx, z))
    for i in ring(ny):
        send(first_b, first_b, 5, dom_at((y + i) % ny, core))
    drain(weights.at[0, core, y, pl.ds(0, nx - 1)], sem_in.at[4])
    then_a = weights.at[0, core, y]
    for i in ring(ny):
        send(then_a, then_a, 6, dom_at((y + i) % ny, core))
    drain(weights.at[1, core, pl.ds(0, ny - 1), x], sem_in.at[5])
    then_b = weights.at[1, core, :, x]
    for i in ring(nx):
        send(then_b, then_b, 7, feat_at((x + i) % nx, z))
    drain(weights.at[0, core, pl.ds(0, ny - 1)], sem_in.at[6])
    drain(weights.at[1, core, :, pl.ds(0, nx - 1)], sem_in.at[7])
    for h in range(2):
        send(weights.at[h, core], weights.at[h, core], 8, dom_at(y, 1 - core))
    drain(by_z.at[0, pl.ds(0, nz - 1), pl.ds(1, nx - 1)], sem_in.at[19])
    drain(ext.at[pl.ds(0, nz - 1)], sem_in.at[21])

    def times_weights(m, own, b):
        total = jnp.zeros((128, 128), F32)
        for h in range(2):
            total = total + lax.dot_general(
                own[h], weights[h, m, b].reshape(depth, 128), (((0,), (0,)), ((), ())),
                preferred_element_type=F32,
            )
        return total

    def rows_of(m, h, b):
        return xm[m, h, :, (b + nx - x) % nx].reshape(band, 128)

    def halves(m):
        return [
            jnp.concatenate([rows_of(m, h, b) for b in range(nx)], axis=0) for h in range(2)
        ]

    drain(weights.at[0], sem_in.at[8])
    own = halves(0)
    for b in range(ny):
        partial[:, b * 128 : (b + 1) * 128] = times_weights(0, own, b)
    drain(by_z.at[1, pl.ds(0, nz - 1)], sem_in.at[20])
    own = halves(1)
    for b in range(ny):
        span = slice(b * 128, (b + 1) * 128)
        value, slope = gelu_pair(partial[:, span] + times_weights(1, own, b))
        hid_ref[:, span] = value.astype(BF)
        grad[:, span] = (cot[:, span].astype(F32) * slope).astype(BF)

    def product_a(m, b):
        return jnp.dot(rows_of(m, 0, b), grad[...], preferred_element_type=F32)

    def product_b(m, b, p):
        columns = grad[:, p * cb * 128 : (p + 1) * cb * 128]
        return jnp.dot(rows_of(m, 1, b), columns, preferred_element_type=F32)

    ca, cb = nx // 2, ny // 2
    for p in range(2):

        def core_a(b, _):
            result = product_a(1 - core, b).astype(BF)
            for c in range(ny):
                other_a[b, c] = result[:, c * 128 : (c + 1) * 128]
            return 0

        def core_b(b, _, p=p):
            result = product_b(1 - core, b, p).astype(BF)
            for c in range(cb):
                other_b[p * cb + c, b] = result[:, c * 128 : (c + 1) * 128]
            return 0

        lax.fori_loop(p * ca, (p + 1) * ca, core_a, 0)
        piece = pl.ds(p * ca, ca)
        send(other_a.at[piece], other_a_in.at[piece], 9 + p, dom_at(y, 1 - core))
        lax.fori_loop(0, nx, core_b, 0)
        piece = pl.ds(p * cb, cb)
        send(other_b.at[piece], other_b_in.at[piece], 11 + p, dom_at(y, 1 - core))

    for p in range(2):

        def y_first(b, _):
            result = product_a(core, b)
            for c in range(ny):
                summed = result[:, c * 128 : (c + 1) * 128] + other_a_in[b, c].astype(F32)
                part_a[c, b] = summed.astype(BF)

                @pl.when(c == y)
                def _():
                    kept_a[b] = summed

            return 0

        def x_first(b, _, p=p):
            result = product_b(core, b, p)
            for c in range(cb):
                column = p * cb + c
                summed = result[:, c * 128 : (c + 1) * 128] + other_b_in[column, b].astype(F32)
                part_b[b, column] = summed.astype(BF)

                @pl.when(b == x)
                def _():
                    kept_b[column] = summed

            return 0

        piece = pl.ds(p * ca, ca)
        drain(other_a_in.at[piece], sem_in.at[9 + p])
        lax.fori_loop(p * ca, (p + 1) * ca, y_first, 0)
        for i in ring(ny):
            c = (y + i) % ny
            send(part_a.at[c, piece], part_a_in.at[y, piece], 13, dom_at(c, core))
        piece = pl.ds(p * cb, cb)
        drain(other_b_in.at[piece], sem_in.at[11 + p])
        lax.fori_loop(0, nx, x_first, 0)
        for i in ring(nx):
            b = (x + i) % nx
            send(part_b.at[b, piece], part_b_in.at[x, piece], 14, feat_at(b, z))

    def y_sum(b):
        total = kept_a[b]
        for j in range(1, ny):
            total = total + part_a_in[(y + j) % ny, b].astype(F32)
        return total

    def x_sum(c):
        total = kept_b[c]
        for j in range(1, nx):
            total = total + part_b_in[(x + j) % nx, c].astype(F32)
        return total

    drain(part_a_in.at[pl.ds(0, ny - 1)], sem_in.at[13])

    def x_then(i, _):
        b = (x + i) % nx
        col_a[b] = y_sum(b).astype(BF)
        send(col_a.at[b], col_a_in.at[x], 15, feat_at(b, z))
        return 0

    lax.fori_loop(1, nx, x_then, 0)
    fin[0] = y_sum(x)

    drain(part_b_in.at[pl.ds(0, nx - 1)], sem_in.at[14])

    def y_then(i, _):
        c = (y + i) % ny
        col_b[c] = x_sum(c).astype(BF)
        send(col_b.at[c], col_b_in.at[y], 16, dom_at(c, core))
        return 0

    lax.fori_loop(1, ny, y_then, 0)
    fin[1] = x_sum(y)

    def z_out(h):
        for i in outward:
            peer = (z + i) % nz

            @pl.when(peer // hz == h)
            def _(peer=peer):
                send(cell.at[peer], cell_in.at[z], 17, feat_at(x, peer))

    drain(col_a_in.at[pl.ds(0, nx - 1)], sem_in.at[15])
    total = fin[0]
    for j in range(1, nx):
        total = total + col_a_in[(x + j) % nx].astype(F32)
    fin[0] = total
    cell[0:hz] = total.astype(BF).reshape(hz, width, 128)
    z_out(0)
    drain(col_b_in.at[pl.ds(0, ny - 1)], sem_in.at[16])
    total = fin[1]
    for j in range(1, ny):
        total = total + col_b_in[(y + j) % ny].astype(F32)
    fin[1] = total
    cell[hz:nz] = total.astype(BF).reshape(hz, width, 128)
    z_out(1)
    drain(cell_in.at[pl.ds(0, nz - 1)], sem_in.at[17])
    total = fin[half, pl.ds(pl.multiple_of(zz * width, width), width)]
    for j in range(1, nz):
        total = total + cell_in[(z + j) % nz].astype(F32)

    final[dom] = total

    def dom_out(i, _):
        send(final.at[dom], final.at[dom], 18, {"feat": feat, "dom": (dom + i) % nd})
        return 0

    lax.fori_loop(1, nd, dom_out, 0)
    drain(final.at[pl.ds(0, nd - 1)], sem_in.at[18])
    for b in range(ny):
        span = slice(b * 128, (b + 1) * 128)
        gs_ref[:, span] = final[b * nc]
        gn_ref[:, span] = final[b * nc + 1]

    sent = (
        halo_out.at[pl.ds(0, nd - 1)], ext.at[pl.ds(0, nz - 1)],
        ext.at[pl.ds(0, (nx - 1) * nz)], mean.at[pl.ds(0, (nx - 1) * nz)], weights.at[0, core, y, pl.ds(0, nx - 1)],
        weights.at[1, core, pl.ds(0, ny - 1), x], weights.at[0, core, pl.ds(0, ny - 1)],
        weights.at[1, core, :, pl.ds(0, nx - 1)], weights.at[0],
        other_a.at[pl.ds(0, nx // 2)], other_a.at[pl.ds(0, nx // 2)],
        other_b.at[pl.ds(0, ny // 2)], other_b.at[pl.ds(0, ny // 2)],
        part_a.at[pl.ds(0, ny - 1)], part_b.at[pl.ds(0, nx - 1)],
        col_a.at[pl.ds(0, nx - 1)], col_b.at[pl.ds(0, ny - 1)], cell.at[pl.ds(0, nz - 1)],
        final.at[pl.ds(0, nd - 1)], by_z.at[0, pl.ds(0, nz - 1), pl.ds(1, nx - 1)],
        by_z.at[1, pl.ds(0, nz - 1)], ext.at[pl.ds(0, nz - 1)],
    )
    for phase, ref in enumerate(sent):
        drain(ref, sem_out.at[phase])


def store_out(hid_in, gs_in, gn_in, hid_ref, gs_ref, gn_ref, hid_buf, gs_buf, gn_buf, sems):
    bufs = (hid_buf, gs_buf, gn_buf)
    ins = [
        pltpu.make_async_copy(a, b, sems.at[i])
        for i, (a, b) in enumerate(zip((hid_in, gs_in, gn_in), bufs))
    ]
    outs = [
        pltpu.make_async_copy(a, b, sems.at[3 + i])
        for i, (a, b) in enumerate(zip(bufs, (hid_ref, gs_ref, gn_ref)))
    ]
    for copy in ins:
        copy.start()
    for i in range(3):
        ins[i].wait()
        outs[i].start()
    for copy in outs:
        copy.wait()


def on_device(features, w1, w2, cotangent, send_rows, send_count, tile_source, tile_kind, patterns):
    nx, nz = FEAT_GRID
    ny, nc = DOM_GRID
    nf, nd, hz = nx * nz, ny * nc, nz // 2
    width = features.shape[1]
    hidden = w1.shape[1]
    slot_tiles = send_rows.shape[2] // 128
    assert features.shape[0] == nf * 128 and hidden == ny * 128 and nc == 2
    band = hz * width
    vmem = pl.BlockSpec(memory_space=pltpu.VMEM)
    hbm = pl.BlockSpec(memory_space=pltpu.HBM)
    source, kind = tile_source[0].T, tile_kind[0].T
    shapes = (
        jax.ShapeDtypeStruct((128, hidden), BF),
        jax.ShapeDtypeStruct((width, hidden), F32),
        jax.ShapeDtypeStruct((width, hidden), F32),
    )
    results = pl.pallas_call(
        layer,
        out_shape=shapes,
        in_specs=[hbm] * 9,
        out_specs=(vmem,) * 3,
        scratch_shapes=[
            pltpu.VMEM((width, nf * 128), BF),
            pltpu.VMEM(send_rows.shape[1:], jnp.int32),
            pltpu.VMEM(patterns.shape, BF),
            pltpu.VMEM((128, hidden), BF),
            pltpu.SMEM(send_count.shape, jnp.int32),
            pltpu.SMEM(source.shape, jnp.int32),
            pltpu.SMEM(kind.shape, jnp.int32),
            pltpu.VMEM((nf + nd * slot_tiles, width, 128), BF),
            pltpu.VMEM((nd, slot_tiles, width, 128), BF),
            pltpu.VMEM((nf, width, 128), BF),
            pltpu.VMEM((2, nz, nx, width, 128), BF),
            pltpu.VMEM((2, 2, hz, nx, width, 128), BF),
            pltpu.VMEM((2, nc, ny, nx, hz, width, 128), BF),
            pltpu.VMEM((128, hidden), F32),
            pltpu.VMEM((128, hidden), BF),
            pltpu.VMEM((nx, ny, band, 128), BF),
            pltpu.VMEM((nx, ny, band, 128), BF),
            pltpu.VMEM((ny, nx, band, 128), BF),
            pltpu.VMEM((ny, nx, band, 128), BF),
            pltpu.VMEM((ny, nx, band, 128), BF),
            pltpu.VMEM((ny, nx, band, 128), BF),
            pltpu.VMEM((nx, ny, band, 128), BF),
            pltpu.VMEM((nx, ny, band, 128), BF),
            pltpu.VMEM((nx, band, 128), F32),
            pltpu.VMEM((ny, band, 128), F32),
            pltpu.VMEM((nx, band, 128), BF),
            pltpu.VMEM((nx, band, 128), BF),
            pltpu.VMEM((ny, band, 128), BF),
            pltpu.VMEM((ny, band, 128), BF),
            pltpu.VMEM((2, band, 128), F32),
            pltpu.VMEM((nz, width, 128), BF),
            pltpu.VMEM((nz, width, 128), BF),
            pltpu.VMEM((nd, width, 128), F32),
            pltpu.SemaphoreType.DMA((22,)),
            pltpu.SemaphoreType.DMA((22,)),
            pltpu.SemaphoreType.DMA((8,)),
            pltpu.SemaphoreType.REGULAR((2,)),
        ],
        compiler_params=pltpu.CompilerParams(
            collective_id=0, has_side_effects=True, vmem_limit_bytes=67_000_000
        ),
    )(
        features.T, w1, w2, cotangent, send_rows, patterns, send_count, source, kind,
    )
    return pl.pallas_call(
        store_out,
        out_shape=shapes,
        in_specs=[hbm] * 3,
        out_specs=(hbm,) * 3,
        scratch_shapes=[pltpu.VMEM(a.shape, a.dtype) for a in shapes]
        + [pltpu.SemaphoreType.DMA((6,))],
        compiler_params=pltpu.CompilerParams(vmem_limit_bytes=67_000_000),
    )(*results)


def solution(mesh):
    placed = (
        P("dom", "feat"),
        P("feat", None),
        P("feat", None),
        P(("dom", "feat"), None),
        P(),
        P(),
        P("dom", None, None),
        P("dom", None, None),
        P(),
    )
    return jax.shard_map(
        on_device,
        mesh=mesh,
        in_specs=placed,
        out_specs=(P(("dom", "feat"), None), P("feat", None), P("feat", None)),
        check_vma=False,
    )
```

```python
import jax
import jax.numpy as jnp
from jax import lax
from jax.experimental import pallas as pl
from jax.experimental.pallas import tpu as pltpu
from jax.sharding import PartitionSpec as P

FEAT_GRID = (4, 16)
DOM_GRID = (4, 2)
inv_root_two = 0.7071067811865476
inv_root_two_pi = 0.3989422804014327
BF = jnp.bfloat16
F32 = jnp.float32
MESH = pl.DeviceIdType.MESH


def gelu_pair(linear):
    normal_cdf = 0.5 * (1.0 + lax.erf(linear * inv_root_two))
    density = jnp.exp(-0.5 * linear * linear) * inv_root_two_pi
    return linear * normal_cdf, normal_cdf + linear * density


def drain(ref, sem):
    pltpu.make_async_copy(ref, ref, sem).wait()


def layer(
    x_hbm, w1_hbm, w2_hbm, cot_hbm, rows_hbm, pat_hbm, count_hbm, source_hbm, kind_hbm,
    hid_ref, gs_ref, gn_ref,
    x_own, wanted_ref, pats, cot, count_ref, source_ref, kind_ref,
    ext, halo_out, mean, by_z, xm, weights, partial, grad, other_a, other_a_in, other_b, other_b_in,
    part_a, part_a_in, part_b, part_b_in, kept_a, kept_b,
    col_a, col_a_in, col_b, col_b_in, fin, cell, cell_in, final,
    sem_out, sem_in, load_sem, round_sem,
):
    nx, nz = FEAT_GRID
    ny, nc = DOM_GRID
    nf, nd, hz = nx * nz, ny * nc, nz // 2
    feat = lax.axis_index("feat")
    dom = lax.axis_index("dom")
    x, z = feat // nz, feat % nz
    y, core = dom // nc, dom % nc
    half, zz = z // hz, z % hz
    width = x_own.shape[0]
    depth = nx * hz * width
    band = hz * width
    tiles = nf
    slot_tiles = halo_out.shape[1]
    slots = wanted_ref.shape[1]
    steps = source_ref.shape[0]

    def send(src, dst, phase, where):
        pltpu.make_async_remote_copy(
            src_ref=src, dst_ref=dst, send_sem=sem_out.at[phase], recv_sem=sem_in.at[phase],
            device_id=where, device_id_type=MESH,
        ).start()

    def feat_at(fx, fz):
        return {"feat": fx * nz + fz, "dom": dom}

    def dom_at(dy, dc):
        return {"feat": feat, "dom": dy * nc + dc}

    block = pl.ds(pl.multiple_of(y * 128, 128), 128)
    my_unit = weights.at[half, core, y, x, zz]
    loads = [
        pltpu.make_async_copy(src, dst, load_sem.at[i])
        for i, (src, dst) in enumerate((
            (x_hbm, x_own), (rows_hbm.at[dom], wanted_ref), (count_hbm, count_ref),
            (pat_hbm, pats), (source_hbm, source_ref), (kind_hbm, kind_ref), (cot_hbm, cot),
        ))
    ]
    barrier = pltpu.get_barrier_semaphore()

    def along(*distances):
        return sorted(({d % nz for d in distances} | {-d % nz for d in distances}) - {0})

    near = along(1, 2)
    for i in near:
        pl.semaphore_signal(barrier, inc=1, device_id=feat_at(x, (z + i) % nz), device_id_type=MESH)
    for i in range(1, nx):
        pl.semaphore_signal(barrier, inc=1, device_id=feat_at((x + i) % nx, z), device_id_type=MESH)
    for i in range(1, nd):
        pl.semaphore_signal(
            barrier, inc=1, device_id={"feat": feat, "dom": (dom + i) % nd}, device_id_type=MESH
        )

    def round_out(r, offsets):
        for i in offsets:
            pl.semaphore_signal(
                round_sem.at[r], inc=1, device_id=feat_at(x, (z + i) % nz), device_id_type=MESH
            )

    for load in loads:
        load.start()

    @pl.when(core == 0)
    def _():
        pltpu.make_async_copy(w1_hbm.at[:, block], my_unit, load_sem.at[7]).start()

    @pl.when(core == 1)
    def _():
        pltpu.make_async_copy(w2_hbm.at[:, block], my_unit, load_sem.at[7]).start()

    for load in loads[:3]:
        load.wait()

    def take(t, _):
        ext[t] = x_own[:, pl.ds(pl.multiple_of(t * 128, 128), 128)]
        return 0

    lax.fori_loop(0, tiles, take, 0)

    group = min(tiles, 16)
    lane_ids = lax.broadcasted_iota(jnp.int32, (128, slots), 0)
    slot_ids = lax.broadcasted_iota(jnp.int32, (1, slots), 1)

    halo_at = tiles + dom * slot_tiles

    def pick(i, _):
        dest = (dom + i) % nd
        wanted = wanted_ref[pl.ds(dest, 1), :]
        low, high = wanted & 127, wanted >> 7
        choose = jnp.where(lane_ids == low, 1.0, 0.0).astype(BF)
        found = jnp.zeros((width, slots), F32)
        for g in range(0, tiles, group):
            rows = ext[g : g + group].reshape(group * width, 128)
            spread = jnp.dot(rows, choose, preferred_element_type=F32)
            for h in range(group):
                found = jnp.where(
                    high == g + h, spread[h * width : (h + 1) * width], found
                )
        live = slot_ids < count_ref[dom, dest]
        found = jnp.where(live, found, 0.0).astype(BF)
        for j in range(slot_tiles):
            halo_out[dest, j] = found[:, j * 128 : (j + 1) * 128]

        @pl.when(dest != dom)
        def _():
            send(
                halo_out.at[dest], ext.at[pl.ds(halo_at, slot_tiles)], 0,
                {"feat": feat, "dom": dest},
            )

        return 0

    def ring(n):
        return sorted(range(1, n), key=lambda i: (-min(i, n - i), i))

    outward = ring(nz)

    def x_send(m, tiles_at, phase, i):
        column = (x + i) % nx
        send(
            tiles_at.at[pl.ds(column * nz, nz)], by_z.at[m, :, nx - i], phase, feat_at(column, z)
        )

    def z_first(least, most):
        for i in outward:
            if least < min(i, nz - i) <= most:
                peer = (z + i) % nz
                send(my_unit, my_unit, 1, feat_at(x, peer))
                send(ext.at[x * nz + peer], xm.at[0, half, zz, 0], 21, feat_at(x, peer))

    assert nz <= 17
    pltpu.make_async_copy(my_unit, my_unit, load_sem.at[7]).wait()
    pl.semaphore_wait(barrier, len(near) + nx - 1 + nd - 1)
    round_out(0, near)
    for i in ring(nx):
        x_send(0, ext, 2, i)
    z_first(0, 2)
    lax.fori_loop(0, nd // 2, pick, 0)
    pl.semaphore_wait(round_sem.at[0], len(near))
    middle = along(4)
    round_out(1, middle)
    z_first(2, 4)
    lax.fori_loop(nd // 2, nd, pick, 0)
    for load in loads[3:]:
        load.wait()
    if middle:
        pl.semaphore_wait(round_sem.at[1], len(middle))
    z_first(4, nz)
    xm[0, half, zz, 0] = ext[feat]
    drain(ext.at[pl.ds(0, (nx - 1) * nz)], sem_in.at[2])
    others = pl.ds(1, nx - 1)
    for i in outward:
        peer = (z + i) % nz
        send(by_z.at[0, peer, others], xm.at[0, half, zz, others], 19, feat_at(x, peer))
    for j in range(1, nx):
        xm[0, half, zz, j] = by_z[0, z, j]
    for j in range(slot_tiles):
        ext[halo_at + j] = halo_out[dom, j]

    ones = jnp.ones((width, 256), BF)

    def mean_of(t):
        total = jnp.zeros((2 * width, 128), F32)
        for k in range(0, steps, 2):
            left = jnp.concatenate([ext[source_ref[k, t]], ext[source_ref[k + 1, t]]], axis=1)
            right = jnp.concatenate([pats[kind_ref[k, t]], pats[kind_ref[k + 1, t]]], axis=1)
            total = total + lax.dot_general(
                jnp.concatenate([left, ones], axis=0), right, (((1,), (1,)), ((), ())),
                preferred_element_type=F32,
            )
        return (total[:width] / total[width : width + 1]).astype(BF)

    drain(ext.at[pl.ds(tiles, (nd - 1) * slot_tiles)], sem_in.at[0])

    def column_means(column):
        def mean_pair(i, _):
            t = column * nz + 2 * i
            first, second = mean_of(t), mean_of(t + 1)
            mean[t] = first
            mean[t + 1] = second
            return 0

        lax.fori_loop(0, nz // 2, mean_pair, 0)

    def column_out(i, _):
        column_means((x + i) % nx)
        x_send(1, mean, 3, i)
        return 0

    lax.fori_loop(1, nx, column_out, 0)
    column_means(x)

    def keep(t, _):
        by_z[1, t, 0] = mean[x * nz + t]
        return 0

    lax.fori_loop(0, nz, keep, 0)
    drain(ext.at[pl.ds(0, nz - 1)], sem_in.at[1])
    first_a, first_b = weights.at[0, core, y, x], weights.at[1, core, y, x]
    for i in ring(nx):
        send(first_a, first_a, 4, feat_at((x + i) % nx, z))
    for i in ring(ny):
        send(first_b, first_b, 5, dom_at((y + i) % ny, core))
    drain(mean.at[pl.ds(0, (nx - 1) * nz)], sem_in.at[3])
    for i in outward:
        peer = (z + i) % nz
        send(by_z.at[1, peer], xm.at[1, half, zz], 20, feat_at(x, peer))
    xm[1, half, zz] = by_z[1, z]

    drain(weights.at[0, core, y, pl.ds(0, nx - 1)], sem_in.at[4])
    then_a = weights.at[0, core, y]
    for i in ring(ny):
        send(then_a, then_a, 6, dom_at((y + i) % ny, core))
    drain(weights.at[1, core, pl.ds(0, ny - 1), x], sem_in.at[5])
    then_b = weights.at[1, core, :, x]
    for i in ring(nx):
        send(then_b, then_b, 7, feat_at((x + i) % nx, z))
    drain(weights.at[0, core, pl.ds(0, ny - 1)], sem_in.at[6])
    drain(weights.at[1, core, :, pl.ds(0, nx - 1)], sem_in.at[7])
    for h in range(2):
        send(weights.at[h, core], weights.at[h, core], 8, dom_at(y, 1 - core))
    drain(by_z.at[0, pl.ds(0, nz - 1), pl.ds(1, nx - 1)], sem_in.at[19])
    drain(ext.at[pl.ds(0, nz - 1)], sem_in.at[21])

    def times_weights(m, own, b):
        total = jnp.zeros((128, 128), F32)
        for h in range(2):
            total = total + lax.dot_general(
                own[h], weights[h, m, b].reshape(depth, 128), (((0,), (0,)), ((), ())),
                preferred_element_type=F32,
            )
        return total

    def rows_of(m, h, b):
        return xm[m, h, :, (b + nx - x) % nx].reshape(band, 128)

    def halves(m):
        return [
            jnp.concatenate([rows_of(m, h, b) for b in range(nx)], axis=0) for h in range(2)
        ]

    drain(weights.at[0], sem_in.at[8])
    own = halves(0)
    for b in range(ny):
        partial[:, b * 128 : (b + 1) * 128] = times_weights(0, own, b)
    drain(by_z.at[1, pl.ds(0, nz - 1)], sem_in.at[20])
    own = halves(1)
    for b in range(ny):
        span = slice(b * 128, (b + 1) * 128)
        value, slope = gelu_pair(partial[:, span] + times_weights(1, own, b))
        hid_ref[:, span] = value.astype(BF)
        grad[:, span] = (cot[:, span].astype(F32) * slope).astype(BF)

    def product_a(m, b):
        return jnp.dot(rows_of(m, 0, b), grad[...], preferred_element_type=F32)

    def product_b(m, b, p):
        columns = grad[:, p * cb * 128 : (p + 1) * cb * 128]
        return jnp.dot(rows_of(m, 1, b), columns, preferred_element_type=F32)

    ca, cb = nx // 2, ny // 2
    for p in range(2):

        def core_a(b, _):
            result = product_a(1 - core, b).astype(BF)
            for c in range(ny):
                other_a[b, c] = result[:, c * 128 : (c + 1) * 128]
            return 0

        def core_b(b, _, p=p):
            result = product_b(1 - core, b, p).astype(BF)
            for c in range(cb):
                other_b[p * cb + c, b] = result[:, c * 128 : (c + 1) * 128]
            return 0

        lax.fori_loop(p * ca, (p + 1) * ca, core_a, 0)
        piece = pl.ds(p * ca, ca)
        send(other_a.at[piece], other_a_in.at[piece], 9 + p, dom_at(y, 1 - core))
        lax.fori_loop(0, nx, core_b, 0)
        piece = pl.ds(p * cb, cb)
        send(other_b.at[piece], other_b_in.at[piece], 11 + p, dom_at(y, 1 - core))

    for p in range(2):

        def y_first(b, _):
            result = product_a(core, b)
            for c in range(ny):
                summed = result[:, c * 128 : (c + 1) * 128] + other_a_in[b, c].astype(F32)
                part_a[c, b] = summed.astype(BF)

                @pl.when(c == y)
                def _():
                    kept_a[b] = summed

            return 0

        def x_first(b, _, p=p):
            result = product_b(core, b, p)
            for c in range(cb):
                column = p * cb + c
                summed = result[:, c * 128 : (c + 1) * 128] + other_b_in[column, b].astype(F32)
                part_b[b, column] = summed.astype(BF)

                @pl.when(b == x)
                def _():
                    kept_b[column] = summed

            return 0

        piece = pl.ds(p * ca, ca)
        drain(other_a_in.at[piece], sem_in.at[9 + p])
        lax.fori_loop(p * ca, (p + 1) * ca, y_first, 0)
        for i in ring(ny):
            c = (y + i) % ny
            send(part_a.at[c, piece], part_a_in.at[y, piece], 13, dom_at(c, core))
        piece = pl.ds(p * cb, cb)
        drain(other_b_in.at[piece], sem_in.at[11 + p])
        lax.fori_loop(0, nx, x_first, 0)
        for i in ring(nx):
            b = (x + i) % nx
            send(part_b.at[b, piece], part_b_in.at[x, piece], 14, feat_at(b, z))

    def y_sum(b):
        total = kept_a[b]
        for j in range(1, ny):
            total = total + part_a_in[(y + j) % ny, b].astype(F32)
        return total

    def x_sum(c):
        total = kept_b[c]
        for j in range(1, nx):
            total = total + part_b_in[(x + j) % nx, c].astype(F32)
        return total

    drain(part_a_in.at[pl.ds(0, ny - 1)], sem_in.at[13])

    def x_then(i, _):
        b = (x + i) % nx
        col_a[b] = y_sum(b).astype(BF)
        send(col_a.at[b], col_a_in.at[x], 15, feat_at(b, z))
        return 0

    lax.fori_loop(1, nx, x_then, 0)
    fin[0] = y_sum(x)

    drain(part_b_in.at[pl.ds(0, nx - 1)], sem_in.at[14])

    def y_then(i, _):
        c = (y + i) % ny
        col_b[c] = x_sum(c).astype(BF)
        send(col_b.at[c], col_b_in.at[y], 16, dom_at(c, core))
        return 0

    lax.fori_loop(1, ny, y_then, 0)
    fin[1] = x_sum(y)

    def z_out(h):
        for i in outward:
            peer = (z + i) % nz

            @pl.when(peer // hz == h)
            def _(peer=peer):
                send(cell.at[peer], cell_in.at[z], 17, feat_at(x, peer))

    drain(col_a_in.at[pl.ds(0, nx - 1)], sem_in.at[15])
    total = fin[0]
    for j in range(1, nx):
        total = total + col_a_in[(x + j) % nx].astype(F32)
    fin[0] = total
    cell[0:hz] = total.astype(BF).reshape(hz, width, 128)
    z_out(0)
    drain(col_b_in.at[pl.ds(0, ny - 1)], sem_in.at[16])
    total = fin[1]
    for j in range(1, ny):
        total = total + col_b_in[(y + j) % ny].astype(F32)
    fin[1] = total
    cell[hz:nz] = total.astype(BF).reshape(hz, width, 128)
    z_out(1)
    drain(cell_in.at[pl.ds(0, nz - 1)], sem_in.at[17])
    total = fin[half, pl.ds(pl.multiple_of(zz * width, width), width)]
    for j in range(1, nz):
        total = total + cell_in[(z + j) % nz].astype(F32)

    final[dom] = total

    def dom_out(i, _):
        send(final.at[dom], final.at[dom], 18, {"feat": feat, "dom": (dom + i) % nd})
        return 0

    lax.fori_loop(1, nd, dom_out, 0)
    drain(final.at[pl.ds(0, nd - 1)], sem_in.at[18])
    for b in range(ny):
        span = slice(b * 128, (b + 1) * 128)
        gs_ref[:, span] = final[b * nc]
        gn_ref[:, span] = final[b * nc + 1]

    sent = (
        halo_out.at[pl.ds(0, nd - 1)], ext.at[pl.ds(0, nz - 1)],
        ext.at[pl.ds(0, (nx - 1) * nz)], mean.at[pl.ds(0, (nx - 1) * nz)], weights.at[0, core, y, pl.ds(0, nx - 1)],
        weights.at[1, core, pl.ds(0, ny - 1), x], weights.at[0, core, pl.ds(0, ny - 1)],
        weights.at[1, core, :, pl.ds(0, nx - 1)], weights.at[0],
        other_a.at[pl.ds(0, nx // 2)], other_a.at[pl.ds(0, nx // 2)],
        other_b.at[pl.ds(0, ny // 2)], other_b.at[pl.ds(0, ny // 2)],
        part_a.at[pl.ds(0, ny - 1)], part_b.at[pl.ds(0, nx - 1)],
        col_a.at[pl.ds(0, nx - 1)], col_b.at[pl.ds(0, ny - 1)], cell.at[pl.ds(0, nz - 1)],
        final.at[pl.ds(0, nd - 1)], by_z.at[0, pl.ds(0, nz - 1), pl.ds(1, nx - 1)],
        by_z.at[1, pl.ds(0, nz - 1)], ext.at[pl.ds(0, nz - 1)],
    )
    for phase, ref in enumerate(sent):
        drain(ref, sem_out.at[phase])


def store_out(hid_in, gs_in, gn_in, hid_ref, gs_ref, gn_ref, hid_buf, gs_buf, gn_buf, sems):
    bufs = (hid_buf, gs_buf, gn_buf)
    ins = [
        pltpu.make_async_copy(a, b, sems.at[i])
        for i, (a, b) in enumerate(zip((hid_in, gs_in, gn_in), bufs))
    ]
    outs = [
        pltpu.make_async_copy(a, b, sems.at[3 + i])
        for i, (a, b) in enumerate(zip(bufs, (hid_ref, gs_ref, gn_ref)))
    ]
    for copy in ins:
        copy.start()
    for i in range(3):
        ins[i].wait()
        outs[i].start()
    for copy in outs:
        copy.wait()


def on_device(features, w1, w2, cotangent, send_rows, send_count, tile_source, tile_kind, patterns):
    nx, nz = FEAT_GRID
    ny, nc = DOM_GRID
    nf, nd, hz = nx * nz, ny * nc, nz // 2
    width = features.shape[1]
    hidden = w1.shape[1]
    slot_tiles = send_rows.shape[2] // 128
    assert features.shape[0] == nf * 128 and hidden == ny * 128 and nc == 2
    band = hz * width
    vmem = pl.BlockSpec(memory_space=pltpu.VMEM)
    hbm = pl.BlockSpec(memory_space=pltpu.HBM)
    source, kind = tile_source[0].T, tile_kind[0].T
    shapes = (
        jax.ShapeDtypeStruct((128, hidden), BF),
        jax.ShapeDtypeStruct((width, hidden), F32),
        jax.ShapeDtypeStruct((width, hidden), F32),
    )
    results = pl.pallas_call(
        layer,
        out_shape=shapes,
        in_specs=[hbm] * 9,
        out_specs=(vmem,) * 3,
        scratch_shapes=[
            pltpu.VMEM((width, nf * 128), BF),
            pltpu.VMEM(send_rows.shape[1:], jnp.int32),
            pltpu.VMEM(patterns.shape, BF),
            pltpu.VMEM((128, hidden), BF),
            pltpu.SMEM(send_count.shape, jnp.int32),
            pltpu.SMEM(source.shape, jnp.int32),
            pltpu.SMEM(kind.shape, jnp.int32),
            pltpu.VMEM((nf + nd * slot_tiles, width, 128), BF),
            pltpu.VMEM((nd, slot_tiles, width, 128), BF),
            pltpu.VMEM((nf, width, 128), BF),
            pltpu.VMEM((2, nz, nx, width, 128), BF),
            pltpu.VMEM((2, 2, hz, nx, width, 128), BF),
            pltpu.VMEM((2, nc, ny, nx, hz, width, 128), BF),
            pltpu.VMEM((128, hidden), F32),
            pltpu.VMEM((128, hidden), BF),
            pltpu.VMEM((nx, ny, band, 128), BF),
            pltpu.VMEM((nx, ny, band, 128), BF),
            pltpu.VMEM((ny, nx, band, 128), BF),
            pltpu.VMEM((ny, nx, band, 128), BF),
            pltpu.VMEM((ny, nx, band, 128), BF),
            pltpu.VMEM((ny, nx, band, 128), BF),
            pltpu.VMEM((nx, ny, band, 128), BF),
            pltpu.VMEM((nx, ny, band, 128), BF),
            pltpu.VMEM((nx, band, 128), F32),
            pltpu.VMEM((ny, band, 128), F32),
            pltpu.VMEM((nx, band, 128), BF),
            pltpu.VMEM((nx, band, 128), BF),
            pltpu.VMEM((ny, band, 128), BF),
            pltpu.VMEM((ny, band, 128), BF),
            pltpu.VMEM((2, band, 128), F32),
            pltpu.VMEM((nz, width, 128), BF),
            pltpu.VMEM((nz, width, 128), BF),
            pltpu.VMEM((nd, width, 128), F32),
            pltpu.SemaphoreType.DMA((22,)),
            pltpu.SemaphoreType.DMA((22,)),
            pltpu.SemaphoreType.DMA((8,)),
            pltpu.SemaphoreType.REGULAR((2,)),
        ],
        compiler_params=pltpu.CompilerParams(
            collective_id=0, has_side_effects=True, vmem_limit_bytes=67_000_000
        ),
    )(
        features.T, w1, w2, cotangent, send_rows, patterns, send_count, source, kind,
    )
    return pl.pallas_call(
        store_out,
        out_shape=shapes,
        in_specs=[hbm] * 3,
        out_specs=(hbm,) * 3,
        scratch_shapes=[pltpu.VMEM(a.shape, a.dtype) for a in shapes]
        + [pltpu.SemaphoreType.DMA((6,))],
        compiler_params=pltpu.CompilerParams(vmem_limit_bytes=67_000_000),
    )(*results)


def solution(mesh):
    placed = (
        P("dom", "feat"),
        P("feat", None),
        P("feat", None),
        P(("dom", "feat"), None),
        P(),
        P(),
        P("dom", None, None),
        P("dom", None, None),
        P(),
    )
    return jax.shard_map(
        on_device,
        mesh=mesh,
        in_specs=placed,
        out_specs=(P(("dom", "feat"), None), P("feat", None), P("feat", None)),
        check_vma=False,
    )
```
